32 devices in a mesh: groups: 2 (over x), ctx: 16 (over z, y, core).
Axes of the slice: x: 2, y: 2, z: 4, core: 2. Of those that a mesh axis runs over, the one named last changes fastest.
Arguments:
- query: bfloat16 [8192, 16, 128], P(('groups', 'ctx')), parts along dimension 0, may hold values from -48 to 48
- query_tangent: bfloat16 [8192, 16, 128], P(('groups', 'ctx')), parts along dimension 0, may hold values from -6 to 6
- keys: bfloat16 [8192, 8, 128], P(('groups', 'ctx')), parts along dimension 0, may hold values from -6 to 6
- values: bfloat16 [8192, 8, 128], P(('groups', 'ctx')), parts along dimension 0, may hold values from -6 to 6
- key_direction: bfloat16 [8192, 8, 128], P(('groups', 'ctx')), parts along dimension 0, may hold values from -6 to 6
- value_direction: bfloat16 [8192, 8, 128], P(('groups', 'ctx')), parts along dimension 0, may hold values from -6 to 6
- out_cotangent: bfloat16 [8192, 16, 128], P(('groups', 'ctx')), parts along dimension 0, may hold values from -6 to 6
- segment_ids: int32 [8192], P(('groups', 'ctx')), parts along dimension 0, may hold values from 0 to 15, never falling along the last dimension, each value on 1 to 1024 neighbouring positions
Outputs:
- key_adjoint: float32 [8192, 8, 128], P(('groups', 'ctx')), parts along dimension 0
- value_adjoint: float32 [8192, 8, 128], P(('groups', 'ctx')), parts along dimension 0
- key_hvp: float32 [8192, 8, 128], P(('groups', 'ctx')), parts along dimension 0
- value_hvp: float32 [8192, 8, 128], P(('groups', 'ctx')), parts along dimension 0
The draws below stay inside these ranges and needn't reach their ends.
There are 2 independent parts, one for each index of `groups`. The reference program is written for one: setup_inputs(seed, part) draws one part's arguments, and reference() takes and returns one part's arrays. A program takes and returns all parts, laid end to end along the dimension named above; each array names one. Nothing has to cross between parts.
Inputs may be any that keep to these rules, and one draw needn't show every extreme that they name: `segment_ids`: segment numbers never fall along the sequence.
All inputs are finite; a program needn't handle non-finite values.
Results may differ from the reference program's by a relative error of at most 0.006.
Values may be sent and summed in bfloat16 or wider, within the bound.
No kernel may reach another device: no remote copies, remote signals or barrier semaphores. Data moves between devices by JAX's collectives and lax.ppermute only.
A program may use at most 128 MiB of HBM per device.

```python
import math
import jax
import jax.numpy as jnp
import numpy as np
from jax import lax

QUERY_HEADS = 16
KEY_VALUE_HEADS = 8
HEAD_WIDTH = 128
WINDOW_LENGTH = 1024
DOCS = 16
TOK_DEV = 256
TOKEN_POSITIONS = 4096


def paired_draw(key):
    first_key_index = jax.random.fold_in(key, 101)
    key_second = jax.random.fold_in(key, 102)
    output_keys = jax.random.truncated_normal(first_key_index, -6.0, 6.0, (TOKEN_POSITIONS, KEY_VALUE_HEADS, HEAD_WIDTH), jnp.float32)
    query_out = jax.random.truncated_normal(key_second, -6.0, 6.0, (TOKEN_POSITIONS, QUERY_HEADS, HEAD_WIDTH), jnp.float32)
    return (query_out, output_keys)


def draw_query(key, part):
    return paired_draw(key)[0].astype(jnp.bfloat16)


def draw_keys(key, part):
    return paired_draw(key)[1].astype(jnp.bfloat16)


def block_levels(stream_key, extent, split, low, high):
    gain, own = 1.0, jax.random.fold_in(stream_key, 6)
    for position, blocks in split:
        steps = jnp.exp(jax.random.uniform(jax.random.fold_in(own, position), (blocks,), jnp.float32, low / len(split), high / len(split)))
        gain = gain * jnp.repeat(steps, extent[position] // blocks).reshape([-1 if axis == position else 1 for axis in range(len(extent))])
    return gain


def profile(amount, total, reach, skew):
    weights = [(1 << 20) // math.isqrt(grade ** skew) + 1 for grade in range(2, amount + 1)]
    spare, holding = total - reach - (amount - 1), [1] * (amount - 1)
    while spare > 0:
        free = [i for i in range(amount - 1) if holding[i] < reach]
        whole, left = sum([weights[i] for i in free]), spare
        for i in free:
            more = min(reach - holding[i], max(1, left * weights[i] // whole), spare)
            holding[i] = holding[i] + more
            spare = spare - more
    return np.array([reach] + holding)


def uneven_parts(rng, count, total, most, slope):
    if count == 2:
        one = jax.random.randint(rng, (), max(1, total - most), min(most, total - 1) + 1)
        return jnp.stack([one, total - one])
    sizes = jnp.asarray(profile(count, total, most, slope), jnp.int32)
    couples = (count - 1) // 2
    giver, taker = sizes[1:1 + 2 * couples:2], sizes[2:2 + 2 * couples:2]
    slack = jnp.minimum(giver - 1, most - taker)
    passed = jax.random.randint(jax.random.fold_in(rng, 1), (couples,), 0, 1 << 20) % (slack + 1)
    sizes = sizes.at[1:1 + 2 * couples:2].set(giver - passed).at[2:2 + 2 * couples:2].set(taker + passed)
    return sizes[jax.random.permutation(jax.random.fold_in(rng, 2), count)]


def centred(own_key, shape, scale, bound, shards=(), kind=jnp.bfloat16):
    values = jax.random.normal(own_key, shape, jnp.float32) * scale
    if len(shards) > 0:
        values = block_levels(own_key, shape, shards, -0.22, 0.18) * values
    return jnp.clip(values, min=-bound, max=bound).astype(kind)


def setup_inputs(seed: int = 0, part: int = 0) -> dict:
    arg_keys = jax.random.split(jax.random.key(seed), 9)
    part_splits = jax.random.split(jax.random.fold_in(arg_keys[8], part), 9)
    return {
        "query": draw_query(jax.random.fold_in(jax.random.fold_in(arg_keys[8], part), 71), part),
        "query_tangent": centred(part_splits[1], (TOKEN_POSITIONS, QUERY_HEADS, HEAD_WIDTH), 1.0, 6.0, ((0, 16),)),
        "keys": draw_keys(jax.random.fold_in(jax.random.fold_in(arg_keys[8], part), 71), part),
        "values": centred(part_splits[3], (TOKEN_POSITIONS, KEY_VALUE_HEADS, HEAD_WIDTH), 1.0, 6.0, ((0, 16),)),
        "key_direction": centred(part_splits[4], (TOKEN_POSITIONS, KEY_VALUE_HEADS, HEAD_WIDTH), 1.0, 6.0, ((0, 16),)),
        "value_direction": centred(part_splits[5], (TOKEN_POSITIONS, KEY_VALUE_HEADS, HEAD_WIDTH), 1.0, 6.0, ((0, 16),)),
        "out_cotangent": centred(part_splits[6], (TOKEN_POSITIONS, QUERY_HEADS, HEAD_WIDTH), 1.0, 6.0, ((0, 16),)),
        "segment_ids": jnp.searchsorted(jnp.cumsum(uneven_parts(part_splits[7], DOCS, TOKEN_POSITIONS, TOKEN_POSITIONS // 4, 1)), jnp.arange(TOKEN_POSITIONS), side="right").astype(jnp.int32),
    }


def contract(matrix, operand):
    return jnp.dot(matrix, operand.T, preferred_element_type=jnp.float32)


def transposed(matrix, operand):
    return jnp.dot(matrix.T, operand, preferred_element_type=jnp.float32)


def band_terms(query_rows, query_dots, cotangent, key_rows, value_rows, key_dots, value_dots, visible):
    factor = query_rows.shape[-1] ** -0.5
    scores = factor * contract(query_rows, key_rows)
    scores_dot = factor * (contract(query_dots, key_rows) + contract(query_rows, key_dots))
    scores = jnp.where(visible, scores, -1e30)
    highest = jnp.max(scores, axis=1, keepdims=True)
    weights = jnp.where(visible, jnp.exp(scores - highest), 0.0)
    mixing = weights / jnp.sum(weights, axis=1, keepdims=True)
    scores_dot = jnp.where(visible, scores_dot, 0.0)
    mixing_dot = mixing * (scores_dot - jnp.sum(mixing * scores_dot, axis=1, keepdims=True))
    upstream = contract(cotangent, value_rows)
    upstream_dot = contract(cotangent, value_dots)
    center = jnp.sum(mixing * upstream, axis=1, keepdims=True)
    center_dot = jnp.sum(mixing_dot * upstream + mixing * upstream_dot, axis=1, keepdims=True)
    grad_scores = mixing * (upstream - center)
    grad_scores_dot = mixing_dot * (upstream - center) + mixing * (upstream_dot - center_dot)
    mixing_b = mixing.astype(jnp.bfloat16)
    mixing_dot_b = mixing_dot.astype(jnp.bfloat16)
    grad_b = grad_scores.astype(jnp.bfloat16)
    grad_dot_b = grad_scores_dot.astype(jnp.bfloat16)
    value_adj = transposed(mixing_b, cotangent)
    value_tan = transposed(mixing_dot_b, cotangent)
    key_adj = factor * transposed(grad_b, query_rows)
    key_tan = factor * (transposed(grad_dot_b, query_rows) + transposed(grad_b, query_dots))
    return key_adj, value_adj, key_tan, value_tan


def band_mask(start, segment_rows, segment_keys, query_group):
    row_count = segment_rows.shape[0]
    width = segment_keys.shape[0]
    query_pos = start + jnp.arange(row_count * query_group, dtype=jnp.int32) // query_group
    key_pos = start - (width - row_count) + jnp.arange(width, dtype=jnp.int32)
    distance = query_pos[:, None] - key_pos[None, :]
    same_doc = jnp.repeat(segment_rows, query_group)[:, None] == segment_keys[None, :]
    return (key_pos[None, :] >= 0) & (distance >= 0) & (distance < WINDOW_LENGTH) & same_doc


def head_terms(query, query_dot, cotangent, key_band, value_band, key_dot, value_dot, visible):
    row_count, head_count, head_size = query.shape
    kv_heads = key_band.shape[1]
    query_group = head_count // kv_heads

    def by_head(array):
        return array.reshape(row_count, kv_heads, query_group, head_size).transpose(1, 0, 2, 3).reshape(kv_heads, row_count * query_group, head_size)

    def by_kv(array):
        return array.transpose(1, 0, 2)

    stacked = (by_head(query), by_head(query_dot), by_head(cotangent), by_kv(key_band), by_kv(value_band), by_kv(key_dot), by_kv(value_dot))
    results = lax.map(lambda items: band_terms(*items, visible), stacked)
    return tuple(result.transpose(1, 0, 2) for result in results)


def reference(query, query_tangent, keys, values, key_direction, value_direction, out_cotangent, segment_ids):
    query_group = QUERY_HEADS // KEY_VALUE_HEADS
    row_total = keys.shape[0]
    block_count = row_total // TOK_DEV

    def padded(array):
        return jnp.concatenate([jnp.zeros((WINDOW_LENGTH,) + array.shape[1:], array.dtype), array], 0)

    key_pad = padded(keys)
    value_pad = padded(values)
    key_dot_pad = padded(key_direction)
    value_dot_pad = padded(value_direction)
    segment_pad = jnp.concatenate([-jnp.ones((WINDOW_LENGTH,), jnp.int32), segment_ids.astype(jnp.int32)], 0)
    width = WINDOW_LENGTH + TOK_DEV

    def one_block(carry, index):
        start = (index * TOK_DEV).astype(jnp.int32)
        query_rows = lax.dynamic_slice_in_dim(query, start, TOK_DEV, 0)
        query_dots = lax.dynamic_slice_in_dim(query_tangent, start, TOK_DEV, 0)
        cotangent = lax.dynamic_slice_in_dim(out_cotangent, start, TOK_DEV, 0)
        key_band = lax.dynamic_slice_in_dim(key_pad, start, width, 0)
        value_band = lax.dynamic_slice_in_dim(value_pad, start, width, 0)
        key_dots = lax.dynamic_slice_in_dim(key_dot_pad, start, width, 0)
        value_dots = lax.dynamic_slice_in_dim(value_dot_pad, start, width, 0)
        segment_keys = lax.dynamic_slice_in_dim(segment_pad, start, width, 0)
        segment_rows = lax.dynamic_slice_in_dim(segment_ids.astype(jnp.int32), start, TOK_DEV, 0)
        visible = band_mask(start, segment_rows, segment_keys, query_group)
        partial_value = head_terms(query_rows, query_dots, cotangent, key_band, value_band, key_dots, value_dots, visible)
        updated = tuple(
            lax.dynamic_update_slice_in_dim(whole, lax.dynamic_slice_in_dim(whole, start, width, 0) + piece, start, 0)
            for whole, piece in zip(carry, partial_value))
        return updated, None

    zero_block = jnp.zeros((WINDOW_LENGTH + row_total, KEY_VALUE_HEADS, HEAD_WIDTH), jnp.float32)
    carry, unused = lax.scan(one_block, (zero_block, zero_block, zero_block, zero_block), jnp.arange(block_count, dtype=jnp.int32))
    return (carry[0][WINDOW_LENGTH:], carry[1][WINDOW_LENGTH:], carry[2][WINDOW_LENGTH:], carry[3][WINDOW_LENGTH:])
```

```python
import functools

import jax
import jax.numpy as jnp
from jax import lax
from jax.experimental import pallas as pl
from jax.experimental.pallas import tpu as pltpu
from jax.sharding import PartitionSpec as P

WINDOW_LENGTH = 1024
HIDDEN = -1e30
TAIL = 16
F32 = jnp.float32
BF16 = jnp.bfloat16


def shifted(block, distance):
    devices = range(lax.axis_size("ctx"))
    route = [(i, i + distance) for i in devices if i + distance in devices]
    return lax.ppermute(block, "ctx", route)


def swapped(block, partner):
    devices = range(lax.axis_size("ctx"))
    return lax.ppermute(block, "ctx", [(i, i ^ partner) for i in devices])


def pack_kernel(plane, heads, group, meta, *refs):
    seg = refs[-1 - plane * heads - 1] if group == 1 else None
    arrays = refs[: len(refs) - 1 - plane * heads - (group == 1)]
    outs = refs[-1 - plane * heads : -1]
    wide = refs[-1]
    me = meta[0]
    for t, array in enumerate(arrays):
        rows, count, width = array.shape
        wide[...] = array[...].astype(F32).reshape(rows * count, width)
        for h in range(heads):
            for k in range(plane):
                first = ((me ^ k) * heads + h) * group
                for g in range(group):
                    at = (t * group + g) * rows
                    outs[h * plane + k][at : at + rows, :] = wide[
                        pl.ds(first + g, rows, stride=count), :
                    ].astype(BF16)
    if group == 1:
        for out in outs:
            out[len(arrays) * rows :, :] = seg[...]


def pack(meta, arrays, plane, heads, group, seg=None):
    rows, count, width = arrays[0].shape
    length = len(arrays) * group * rows + (0 if seg is None else TAIL)
    vmem = pl.BlockSpec(memory_space=pltpu.VMEM)
    inputs = list(arrays) + ([] if seg is None else [seg])
    return pl.pallas_call(
        functools.partial(pack_kernel, plane, heads, group),
        out_shape=[jax.ShapeDtypeStruct((length, width), BF16)] * (plane * heads),
        in_specs=[pl.BlockSpec(memory_space=pltpu.SMEM)] + [vmem] * len(inputs),
        out_specs=[vmem] * (plane * heads),
        scratch_shapes=[pltpu.VMEM((rows * count, width), F32)],
        name="pack",
    )(meta, *inputs)


def attend_kernel(plane, group, rows, width, meta, *refs):
    own, prev, queries = refs[:plane], refs[plane : 2 * plane], refs[2 * plane : 3 * plane]
    out_prev, out_own = refs[3 * plane : 4 * plane], refs[4 * plane : 5 * plane]
    ka, kd, vv, segs, qq, do, qt, qa, dt, s, sd, u, ud, acc, tri, lims, sem = refs[5 * plane :]
    me, valid = meta[0], meta[1]
    span = group * rows
    factor = width ** (-0.5)
    slope = factor * 1.4426950408889634

    copies = []

    def fetch(source, target):
        copy = pltpu.make_async_copy(source, target, sem.at[len(copies)])
        copy.start()
        copies.append(copy)

    low, high = pl.ds(0, width), pl.ds(width, width)
    for k in range(plane):
        for piece, base in ((own[k], plane), (prev[k], 0)):
            block = base + (me ^ k)
            part = [piece.at[pl.ds(t * rows, rows), :] for t in range(4)]
            fetch(part[0], ka.at[block, :, low])
            fetch(part[0], kd.at[block, :, high])
            fetch(part[1], vv.at[block, 0])
            fetch(part[2], kd.at[block, :, low])
            fetch(part[3], vv.at[block, 1])
            fetch(piece.at[pl.ds(4 * rows, TAIL), :], segs.at[block])
        block = me ^ k
        part = [queries[k].at[pl.ds(t * span, span), :] for t in range(3)]
        fetch(part[0], qq.at[block, :, low])
        fetch(part[1], qq.at[block, :, high])
        fetch(part[2], do.at[block])
    key_at = lax.broadcasted_iota(jnp.int32, (rows, rows), 0)
    row_at = lax.broadcasted_iota(jnp.int32, (rows, rows), 1)
    for g in range(group):
        lanes = slice(g * rows, (g + 1) * rows)
        tri[0, :, lanes] = jnp.where(key_at > row_at, 0.0, HIDDEN)
        tri[1, :, lanes] = jnp.where(key_at <= row_at, 0.0, HIDDEN)
    acc[...] = jnp.zeros_like(acc)
    for copy in copies:
        copy.wait()

    lane_rows = rows // width

    def document_row(block):
        tail = segs[block].astype(F32)
        return jnp.concatenate([tail[r : r + 1, :] for r in range(lane_rows)], axis=1)

    names = lax.broadcasted_iota(jnp.int32, (width, rows), 0).astype(F32)
    for block in range(2 * plane):
        docs = document_row(block)
        hot = jnp.where(names == docs, 1.0, 0.0)
        ka[block, :, width:] = hot.T.astype(BF16)
        last = jnp.max(docs)
        lims[0, block] = jnp.min(docs)
        lims[1, block] = jnp.where(valid > 0, last, -1.0) if block < plane else last

    def folded(values):
        return values.reshape(rows // 8, 8, span)

    def one_block(a, carry):
        first = lims[0, plane + a]
        skip = sum((lims[1, a + b] < first).astype(jnp.int32) for b in range(plane))
        both = qq[a].astype(F32).T.astype(BF16)
        qt[...] = both
        qa[:width, :] = both[:width, :]
        docs = document_row(plane + a)
        cover = jnp.where(names == docs, 0.0, HIDDEN).astype(BF16)
        for g in range(group):
            qa[width:, g * rows : (g + 1) * rows] = cover
        dt[...] = do[a].astype(F32).T.astype(BF16)

        def score(b, bias, top):
            value = jnp.dot(ka[a + b], qa[...], preferred_element_type=F32)
            if bias is not None:
                value = value + tri[bias]
            s[b] = value
            return jnp.maximum(top, jnp.max(folded(value), axis=0))

        top = jnp.full((8, span), HIDDEN, F32)
        top = score(plane, 1, top)
        top = lax.fori_loop(jnp.maximum(skip, 1), plane, lambda b, t: score(b, None, t), top)
        top = lax.cond(skip == 0, lambda t: score(0, 0, t), lambda t: t, top)
        peak = slope * jnp.max(top, axis=0, keepdims=True)

        def sums(b, carry):
            total, dots, ups, both = carry
            weight = jnp.exp2(slope * s[b] - peak)
            s[b] = weight
            dot = factor * jnp.dot(kd[a + b], qt[...], preferred_element_type=F32)
            sd[b] = dot
            up = jnp.dot(vv[a + b, 0], dt[...], preferred_element_type=F32)
            u[b] = up
            updot = jnp.dot(vv[a + b, 1], dt[...], preferred_element_type=F32)
            ud[b] = updot
            total = total + jnp.sum(folded(weight), axis=0)
            dots = dots + jnp.sum(folded(weight * dot), axis=0)
            ups = ups + jnp.sum(folded(weight * up), axis=0)
            both = both + jnp.sum(folded(weight * (dot * up + updot)), axis=0)
            return total, dots, ups, both

        zero = jnp.zeros((8, span), F32)
        carried = lax.fori_loop(skip, plane + 1, sums, (zero, zero, zero, zero))
        total, dots, ups, both = (jnp.sum(x, axis=0, keepdims=True) for x in carried)
        share = 1.0 / total
        mean_dot = dots * share
        center = ups * share
        center_dot = both * share - mean_dot * center

        def adjoints(b, carry):
            mix = s[b] * share
            dot = sd[b] - mean_dot
            up = u[b] - center
            mix_dot = mix * dot
            grad = mix * up
            grad_dot = mix * (dot * up + (ud[b] - center_dot))
            mix_b, mix_dot_b = mix.astype(BF16), mix_dot.astype(BF16)
            grad_b, grad_dot_b = grad.astype(BF16), grad_dot.astype(BF16)
            cot = do[a]
            pair = jnp.dot(grad_b, qq[a], preferred_element_type=F32)
            acc[a + b, 0] += pair[:, :width]
            acc[a + b, 1] += jnp.dot(mix_b, cot, preferred_element_type=F32)
            acc[a + b, 2] += pair[:, width:] + jnp.dot(
                grad_dot_b, qq[a, :, :width], preferred_element_type=F32
            )
            acc[a + b, 3] += jnp.dot(mix_dot_b, cot, preferred_element_type=F32)
            return carry

        lax.fori_loop(skip, plane + 1, adjoints, 0)
        return carry

    lax.fori_loop(0, plane, one_block, 0)
    for k in range(plane):
        for t in range(4):
            scale = factor if t % 2 == 0 else 1.0
            at = slice(t * rows, (t + 1) * rows)
            out_prev[k][at, :] = (scale * acc[me ^ k, t]).astype(BF16)
            out_own[k][at, :] = scale * acc[plane + (me ^ k), t]


def attend(meta, own, prev, queries, plane, group):
    length, width = own[0].shape
    rows = (length - TAIL) // 4
    span = group * rows
    vmem = pl.BlockSpec(memory_space=pltpu.VMEM)
    blocks = 2 * plane
    results = pl.pallas_call(
        functools.partial(attend_kernel, plane, group, rows, width),
        out_shape=[jax.ShapeDtypeStruct((4 * rows, width), BF16)] * plane
        + [jax.ShapeDtypeStruct((4 * rows, width), F32)] * plane,
        in_specs=[pl.BlockSpec(memory_space=pltpu.SMEM)]
        + [pl.BlockSpec(memory_space=pl.ANY)] * (3 * plane),
        out_specs=[vmem] * (2 * plane),
        scratch_shapes=[
            pltpu.VMEM((blocks, rows, 2 * width), BF16),
            pltpu.VMEM((blocks, rows, 2 * width), BF16),
            pltpu.VMEM((blocks, 2, rows, width), BF16),
            pltpu.VMEM((blocks, TAIL, width), BF16),
            pltpu.VMEM((plane, span, 2 * width), BF16),
            pltpu.VMEM((plane, span, width), BF16),
            pltpu.VMEM((2 * width, span), BF16),
            pltpu.VMEM((2 * width, span), BF16),
            pltpu.VMEM((width, span), BF16),
        ]
        + [pltpu.VMEM((plane + 1, rows, span), F32)] * 4
        + [
            pltpu.VMEM((blocks, 4, rows, width), F32),
            pltpu.VMEM((2, rows, span), F32),
            pltpu.SMEM((2, blocks), F32),
            pltpu.SemaphoreType.DMA((15 * plane,)),
        ],
        name="attend",
    )(meta, *own, *prev, *queries)
    return results[:plane], results[plane:]


def finish_kernel(plane, heads, meta, *refs):
    pieces, returned = refs[: plane * heads], refs[plane * heads : plane * heads + heads]
    outs = refs[-4:]
    me = meta[0]
    for h in range(heads):
        for k in range(plane):
            piece = pieces[h * plane + k]
            rows = piece.shape[0] // 4
            head = (me ^ k) * heads + h
            for t in range(4):
                at = slice(t * rows, (t + 1) * rows)
                value = piece[at, :].astype(F32)
                if k == 0:
                    value = value + returned[h][at, :].astype(F32)
                outs[t][pl.ds(head, rows, stride=plane * heads), :] = value


def finish(meta, pieces, returned, plane, heads):
    length, width = pieces[0].shape
    vmem = pl.BlockSpec(memory_space=pltpu.VMEM)
    return pl.pallas_call(
        functools.partial(finish_kernel, plane, heads),
        out_shape=[jax.ShapeDtypeStruct((length // 4 * plane * heads, width), F32)] * 4,
        in_specs=[pl.BlockSpec(memory_space=pltpu.SMEM)] + [vmem] * (plane * heads + heads),
        out_specs=[vmem] * 4,
        name="finish",
    )(meta, *pieces, *returned)


def local(
    query, query_tangent, keys, values, key_direction, value_direction, out_cotangent, segment_ids
):
    rows, kv_heads, width = keys.shape
    group = query.shape[1] // kv_heads
    plane = WINDOW_LENGTH // rows
    heads = kv_heads // plane
    device = lax.axis_index("ctx")
    meta = jnp.stack([device % plane, device // plane]).astype(jnp.int32)
    seg = jnp.zeros((TAIL, width), BF16)
    seg = seg.at[: rows // width].set(segment_ids.reshape(rows // width, width).astype(BF16))
    kv = pack(meta, (keys, values, key_direction, value_direction), plane, heads, 1, seg)
    qs = pack(meta, (query, query_tangent, out_cotangent), plane, heads, group)

    pieces, returned = [], []
    for h in range(heads):
        own = [kv[h * plane]] + [swapped(kv[h * plane + k], k) for k in range(1, plane)]
        prev = [shifted(own[k], plane) for k in range(plane)]
        queries = [qs[h * plane]] + [swapped(qs[h * plane + k], k) for k in range(1, plane)]
        sums_prev, sums_own = attend(meta, own, prev, queries, plane, group)
        back = [shifted(sums_prev[k], -plane) for k in range(plane)]
        returned.append(back[0])
        pieces.append(sums_own[0])
        for k in range(1, plane):
            pieces.append(swapped((sums_own[k] + back[k].astype(F32)).astype(BF16), k))
    outs = finish(meta, pieces, returned, plane, heads)
    return tuple(out.reshape(rows, kv_heads, width) for out in outs)


def solution(mesh):
    whole = P(("groups", "ctx"), None, None)
    return jax.shard_map(
        local,
        mesh=mesh,
        in_specs=(whole,) * 7 + (P(("groups", "ctx")),),
        out_specs=(whole,) * 4,
        check_vma=False,
    )
```

```python
import functools

import jax
import jax.numpy as jnp
from jax import lax
from jax.experimental import pallas as pl
from jax.experimental.pallas import tpu as pltpu
from jax.sharding import PartitionSpec as P


WINDOW_LENGTH = 1024
HIDDEN = -1e30
TAIL = 16
F32 = jnp.float32
BF16 = jnp.bfloat16


def shifted(block, distance):
    devices = range(lax.axis_size("ctx"))
    route = [(i, i + distance) for i in devices if i + distance in devices]
    return lax.ppermute(block, "ctx", route)


def swapped(block, partner):
    devices = range(lax.axis_size("ctx"))
    return lax.ppermute(block, "ctx", [(i, i ^ partner) for i in devices])


def pack_kernel(plane, heads, group, arrays, *refs):
    seg = refs[arrays] if group == 1 else None
    outs, wide = refs[-1 - plane * heads : -1], refs[-1]
    me = lax.rem(lax.axis_index("ctx"), plane)
    for t, array in enumerate(refs[:arrays]):
        rows, count, width = array.shape
        wide[...] = array[...].astype(F32).reshape(rows * count, width)
        for h in range(heads):
            for k in range(plane):
                first = ((me ^ k) * heads + h) * group
                for g in range(group):
                    at = (t * group + g) * rows
                    outs[h * plane + k][at : at + rows, :] = wide[
                        pl.ds(first + g, rows, stride=count), :
                    ].astype(BF16)
    if group == 1:
        docs = seg[...].astype(F32)
        filler = jnp.zeros((TAIL - docs.shape[0], docs.shape[1]), F32)
        tail = jnp.concatenate([docs, filler], axis=0).astype(BF16)
        for out in outs:
            out[arrays * rows :, :] = tail


def pack(arrays, plane, heads, group, seg=None):
    rows, count, width = arrays[0].shape
    length = len(arrays) * group * rows + (0 if seg is None else TAIL)
    vmem = pl.BlockSpec(memory_space=pltpu.VMEM)
    inputs = list(arrays) + ([] if seg is None else [seg])
    return pl.pallas_call(
        functools.partial(pack_kernel, plane, heads, group, len(arrays)),
        out_shape=[jax.ShapeDtypeStruct((length, width), BF16)] * (plane * heads),
        in_specs=[vmem] * len(inputs),
        out_specs=[vmem] * (plane * heads),
        scratch_shapes=[pltpu.VMEM((rows * count, width), F32)],
        name="pack",
    )(*inputs)


def attend_kernel(plane, group, rows, width, *refs):
    half = plane // 2
    length = 4 * rows + TAIL
    own, pairs, queries = refs[:plane], refs[plane : plane + 2], refs[plane + 2 : 2 * plane + 2]
    out_prev, out_own = refs[2 * plane + 2 : 2 * plane + 4], refs[2 * plane + 4 : 3 * plane + 4]
    ka, kd, vv, segs, qq, do, qt, qa, dt, s, sd, u, ud, acc, tri, lims, sem = refs[3 * plane + 4 :]
    device = lax.axis_index("ctx")
    me = lax.rem(device, plane)
    span = group * rows
    factor = width ** (-0.5)
    slope = factor * 1.4426950408889634

    copies = []

    def fetch(source, target):
        copy = pltpu.make_async_copy(source, target, sem.at[len(copies)])
        copy.start()
        copies.append(copy)

    low, high = pl.ds(0, width), pl.ds(width, width)
    for k in range(plane):
        for piece, start, base in ((own[k], 0, plane), (pairs[k // half], k % half * length, 0)):
            block = base + (me ^ k)
            part = [piece.at[pl.ds(start + t * rows, rows), :] for t in range(4)]
            fetch(part[0], ka.at[block, :, low])
            fetch(part[0], kd.at[block, :, high])
            fetch(part[1], vv.at[block, 0])
            fetch(part[2], kd.at[block, :, low])
            fetch(part[3], vv.at[block, 1])
            fetch(piece.at[pl.ds(start + 4 * rows, TAIL), :], segs.at[block])
        block = me ^ k
        part = [queries[k].at[pl.ds(t * span, span), :] for t in range(3)]
        fetch(part[0], qq.at[block, :, low])
        fetch(part[1], qq.at[block, :, high])
        fetch(part[2], do.at[block])
    key_at = lax.broadcasted_iota(jnp.int32, (rows, rows), 0)
    row_at = lax.broadcasted_iota(jnp.int32, (rows, rows), 1)
    for g in range(group):
        lanes = slice(g * rows, (g + 1) * rows)
        tri[0, :, lanes] = jnp.where(key_at > row_at, 0.0, HIDDEN)
        tri[1, :, lanes] = jnp.where(key_at <= row_at, 0.0, HIDDEN)
    acc[...] = jnp.zeros_like(acc)
    for copy in copies:
        copy.wait()

    lane_rows = rows // width

    def document_row(block):
        tail = segs[block].astype(F32)
        return jnp.concatenate([tail[r : r + 1, :] for r in range(lane_rows)], axis=1)

    names = lax.broadcasted_iota(jnp.int32, (width, rows), 0).astype(F32)
    for block in range(2 * plane):
        docs = document_row(block)
        hot = jnp.where(names == docs, 1.0, 0.0)
        ka[block, :, width:] = hot.T.astype(BF16)
        last = jnp.max(docs)
        lims[0, block] = jnp.min(docs)
        lims[1, block] = jnp.where(device >= plane, last, -1.0) if block < plane else last

    def folded(values):
        return values.reshape(rows // 8, 8, span)

    def one_block(a, carry):
        first = lims[0, plane + a]
        skip = sum((lims[1, a + b] < first).astype(jnp.int32) for b in range(plane))
        both = qq[a].astype(F32).T.astype(BF16)
        qt[...] = both
        qa[:width, :] = both[:width, :]
        docs = document_row(plane + a)
        cover = jnp.where(names == docs, 0.0, HIDDEN).astype(BF16)
        for g in range(group):
            qa[width:, g * rows : (g + 1) * rows] = cover
        dt[...] = do[a].astype(F32).T.astype(BF16)

        def score(b, bias, top):
            value = jnp.dot(ka[a + b], qa[...], preferred_element_type=F32)
            if bias is not None:
                value = value + tri[bias]
            s[b] = value
            return jnp.maximum(top, jnp.max(folded(value), axis=0))

        top = jnp.full((8, span), HIDDEN, F32)
        top = score(plane, 1, top)
        top = lax.fori_loop(jnp.maximum(skip, 1), plane, lambda b, t: score(b, None, t), top)
        top = lax.cond(skip == 0, lambda t: score(0, 0, t), lambda t: t, top)
        peak = slope * jnp.max(top, axis=0, keepdims=True)

        def sums(b, carry):
            total, dots, ups, both = carry
            weight = jnp.exp2(slope * s[b] - peak)
            s[b] = weight
            dot = factor * jnp.dot(kd[a + b], qt[...], preferred_element_type=F32)
            sd[b] = dot
            up = jnp.dot(vv[a + b, 0], dt[...], preferred_element_type=F32)
            u[b] = up
            updot = jnp.dot(vv[a + b, 1], dt[...], preferred_element_type=F32)
            ud[b] = updot
            total = total + jnp.sum(folded(weight), axis=0)
            dots = dots + jnp.sum(folded(weight * dot), axis=0)
            ups = ups + jnp.sum(folded(weight * up), axis=0)
            both = both + jnp.sum(folded(weight * (dot * up + updot)), axis=0)
            return total, dots, ups, both

        zero = jnp.zeros((8, span), F32)
        carried = lax.fori_loop(skip, plane + 1, sums, (zero, zero, zero, zero))
        total, dots, ups, both = (jnp.sum(x, axis=0, keepdims=True) for x in carried)
        share = 1.0 / total
        mean_dot = dots * share
        center = ups * share
        center_dot = both * share - mean_dot * center

        def adjoints(b, carry):
            mix = s[b] * share
            dot = sd[b] - mean_dot
            up = u[b] - center
            mix_dot = mix * dot
            grad = mix * up
            grad_dot = mix * (dot * up + (ud[b] - center_dot))
            mix_b, mix_dot_b = mix.astype(BF16), mix_dot.astype(BF16)
            grad_b, grad_dot_b = grad.astype(BF16), grad_dot.astype(BF16)
            cot = do[a]
            pair = jnp.dot(grad_b, qq[a], preferred_element_type=F32)
            acc[a + b, 0] += pair[:, :width]
            acc[a + b, 1] += jnp.dot(mix_b, cot, preferred_element_type=F32)
            acc[a + b, 2] += pair[:, width:] + jnp.dot(
                grad_dot_b, qq[a, :, :width], preferred_element_type=F32
            )
            acc[a + b, 3] += jnp.dot(mix_dot_b, cot, preferred_element_type=F32)
            return carry

        lax.fori_loop(skip, plane + 1, adjoints, 0)
        return carry

    lax.fori_loop(0, plane, one_block, 0)
    for k in range(plane):
        for t in range(4):
            scale = factor if t % 2 == 0 else 1.0
            at = slice(t * rows, (t + 1) * rows)
            there = slice((k % half * 4 + t) * rows, (k % half * 4 + t + 1) * rows)
            out_prev[k // half][there, :] = (scale * acc[me ^ k, t]).astype(BF16)
            out_own[k][at, :] = scale * acc[plane + (me ^ k), t]


def attend(own, pairs, queries, plane, group):
    length, width = own[0].shape
    rows = (length - TAIL) // 4
    span = group * rows
    vmem = pl.BlockSpec(memory_space=pltpu.VMEM)
    blocks = 2 * plane
    results = pl.pallas_call(
        functools.partial(attend_kernel, plane, group, rows, width),
        out_shape=[jax.ShapeDtypeStruct((2 * plane * rows, width), BF16)] * 2
        + [jax.ShapeDtypeStruct((4 * rows, width), F32)] * plane,
        in_specs=[pl.BlockSpec(memory_space=pl.ANY)] * (2 * plane + 2),
        out_specs=[vmem] * (plane + 2),
        scratch_shapes=[
            pltpu.VMEM((blocks, rows, 2 * width), BF16),
            pltpu.VMEM((blocks, rows, 2 * width), BF16),
            pltpu.VMEM((blocks, 2, rows, width), BF16),
            pltpu.VMEM((blocks, TAIL, width), BF16),
            pltpu.VMEM((plane, span, 2 * width), BF16),
            pltpu.VMEM((plane, span, width), BF16),
            pltpu.VMEM((2 * width, span), BF16),
            pltpu.VMEM((2 * width, span), BF16),
            pltpu.VMEM((width, span), BF16),
        ]
        + [pltpu.VMEM((plane + 1, rows, span), F32)] * 4
        + [
            pltpu.VMEM((blocks, 4, rows, width), F32),
            pltpu.VMEM((2, rows, span), F32),
            pltpu.SMEM((2, blocks), F32),
            pltpu.SemaphoreType.DMA((15 * plane,)),
        ],
        name="attend",
    )(*own, *pairs, *queries)
    return results[:2], results[2:]


def finish_kernel(plane, heads, *refs):
    pieces, returned = refs[: plane * heads], refs[plane * heads : plane * heads + heads]
    outs = refs[-4:]
    me = lax.rem(lax.axis_index("ctx"), plane)
    for h in range(heads):
        for k in range(plane):
            piece = pieces[h * plane + k]
            rows = piece.shape[0] // 4
            head = (me ^ k) * heads + h
            for t in range(4):
                at = slice(t * rows, (t + 1) * rows)
                value = piece[at, :].astype(F32)
                if k == 0:
                    value = value + returned[h][at, :].astype(F32)
                outs[t][pl.ds(head, rows, stride=plane * heads), :] = value


def finish(pieces, returned, plane, heads):
    length, width = pieces[0].shape
    vmem = pl.BlockSpec(memory_space=pltpu.VMEM)
    return pl.pallas_call(
        functools.partial(finish_kernel, plane, heads),
        out_shape=[jax.ShapeDtypeStruct((length // 4 * plane * heads, width), F32)] * 4,
        in_specs=[vmem] * (plane * heads + heads),
        out_specs=[vmem] * 4,
        name="finish",
    )(*pieces, *returned)


def local(
    query, query_tangent, keys, values, key_direction, value_direction, out_cotangent, segment_ids
):
    rows, kv_heads, width = keys.shape
    group = query.shape[1] // kv_heads
    plane = WINDOW_LENGTH // rows
    half = plane // 2
    heads = kv_heads // plane
    far_first = list(range(half, plane)) + list(range(1, half))

    def spread(blocks, h):
        results = [blocks[h * plane]] + [None] * (plane - 1)
        for k in far_first:
            results[k] = swapped(blocks[h * plane + k], k)
        return results

    seg = segment_ids.reshape(rows // width, width)
    kv = pack((keys, values, key_direction, value_direction), plane, heads, 1, seg)
    qs = pack((query, query_tangent, out_cotangent), plane, heads, group)
    pieces, returned = [], []
    for h in range(heads):
        own = spread(kv, h)
        pairs = []
        for part in (own[:half], own[half:]):
            pairs.append(shifted(jnp.concatenate(part, axis=0), plane))
        queries = spread(qs, h)
        sums_prev, sums_own = attend(own, pairs, queries, plane, group)
        back = [None, None]
        for i in (1, 0):
            back[i] = shifted(sums_prev[i], -plane)
        returned.append(back[0])
        totals = [sums_own[0]]
        for k in range(1, plane):
            at = slice(k % half * 4 * rows, (k % half + 1) * 4 * rows)
            totals.append((sums_own[k] + back[k // half][at].astype(F32)).astype(BF16))
        results = [totals[0]] + [None] * (plane - 1)
        for k in far_first:
            results[k] = swapped(totals[k], k)
        pieces.extend(results)
    outs = finish(pieces, returned, plane, heads)
    return tuple(out.reshape(rows, kv_heads, width) for out in outs)


def solution(mesh):
    whole = P(("groups", "ctx"), None, None)
    return jax.shard_map(
        local,
        mesh=mesh,
        in_specs=(whole,) * 7 + (P(("groups", "ctx")),),
        out_specs=(whole,) * 4,
        check_vma=False,
    )
```

```python
import functools

import jax
import jax.numpy as jnp
from jax import lax
from jax.experimental import pallas as pl
from jax.experimental.pallas import tpu as pltpu
from jax.sharding import PartitionSpec as P


WINDOW_LENGTH = 1024
HIDDEN = -1e30
TAIL = 16
F32 = jnp.float32
BF16 = jnp.bfloat16


def shifted(block, distance):
    devices = range(lax.axis_size("ctx"))
    route = [(i, i + distance) for i in devices if i + distance in devices]
    return lax.ppermute(block, "ctx", route)


def swapped(block, partner):
    devices = range(lax.axis_size("ctx"))
    return lax.ppermute(block, "ctx", [(i, i ^ partner) for i in devices])


def pack_kernel(plane, heads, group, arrays, *refs):
    seg = refs[arrays] if group == 1 else None
    outs, wide = refs[-2 - (plane - 1) * heads : -1], refs[-1]
    length = outs[1].shape[0]
    me = lax.rem(lax.axis_index("ctx"), plane)
    for t, array in enumerate(refs[:arrays]):
        rows, count, width = array.shape
        wide[...] = array[...].astype(F32).reshape(rows * count, width)
        for h in range(heads):
            for k in range(plane):
                first = ((me ^ k) * heads + h) * group
                out = outs[0] if k == 0 else outs[h * (plane - 1) + k]
                for g in range(group):
                    at = (t * group + g) * rows + (h * length if k == 0 else 0)
                    out[at : at + rows, :] = wide[
                        pl.ds(first + g, rows, stride=count), :
                    ].astype(BF16)
    if group == 1:
        docs = seg[...].astype(F32)
        filler = jnp.zeros((TAIL - docs.shape[0], docs.shape[1]), F32)
        tail = jnp.concatenate([docs, filler], axis=0).astype(BF16)
        for h in range(heads):
            outs[0][(h + 1) * length - TAIL : (h + 1) * length, :] = tail
        for out in outs[1:]:
            out[length - TAIL :, :] = tail


def pack(arrays, plane, heads, group, seg=None):
    rows, count, width = arrays[0].shape
    length = len(arrays) * group * rows + (0 if seg is None else TAIL)
    vmem = pl.BlockSpec(memory_space=pltpu.VMEM)
    inputs = list(arrays) + ([] if seg is None else [seg])
    pieces = (plane - 1) * heads
    return pl.pallas_call(
        functools.partial(pack_kernel, plane, heads, group, len(arrays)),
        out_shape=[jax.ShapeDtypeStruct((heads * length, width), BF16)]
        + [jax.ShapeDtypeStruct((length, width), BF16)] * pieces,
        in_specs=[vmem] * len(inputs),
        out_specs=[vmem] * (1 + pieces),
        scratch_shapes=[pltpu.VMEM((rows * count, width), F32)],
        name="pack",
    )(*inputs)


def attend_kernel(plane, group, rows, width, head, *refs):
    half = plane // 2
    length = 4 * rows + TAIL
    own, pairs, queries = refs[:plane], refs[plane : plane + 2], refs[plane + 2 : 2 * plane + 2]
    out_prev, out_own = refs[2 * plane + 2 : 2 * plane + 4], refs[2 * plane + 4 : 3 * plane + 4]
    ka, kd, vv, segs, qq, do, qt, qa, dt, s, sd, u, ud, acc, tri, lims, sem = refs[3 * plane + 4 :]
    device = lax.axis_index("ctx")
    me = lax.rem(device, plane)
    span = group * rows
    factor = width ** (-0.5)
    slope = factor * 1.4426950408889634

    copies = []

    def fetch(source, target):
        copy = pltpu.make_async_copy(source, target, sem.at[len(copies)])
        copy.start()
        copies.append(copy)

    low, high = pl.ds(0, width), pl.ds(width, width)
    for k in range(plane):
        mine = (own[k], head * length if k == 0 else 0, plane)
        past = (pairs[min(k, 1)], (head if k == 0 else k - 1) * length, 0)
        for piece, start, base in (mine, past):
            block = base + (me ^ k)
            part = [piece.at[pl.ds(start + t * rows, rows), :] for t in range(4)]
            fetch(part[0], ka.at[block, :, low])
            fetch(part[0], kd.at[block, :, high])
            fetch(part[1], vv.at[block, 0])
            fetch(part[2], kd.at[block, :, low])
            fetch(part[3], vv.at[block, 1])
            fetch(piece.at[pl.ds(start + 4 * rows, TAIL), :], segs.at[block])
        block = me ^ k
        start = head * 3 * span if k == 0 else 0
        part = [queries[k].at[pl.ds(start + t * span, span), :] for t in range(3)]
        fetch(part[0], qq.at[block, :, low])
        fetch(part[1], qq.at[block, :, high])
        fetch(part[2], do.at[block])
    key_at = lax.broadcasted_iota(jnp.int32, (rows, rows), 0)
    row_at = lax.broadcasted_iota(jnp.int32, (rows, rows), 1)
    for g in range(group):
        lanes = slice(g * rows, (g + 1) * rows)
        tri[0, :, lanes] = jnp.where(key_at > row_at, 0.0, HIDDEN)
        tri[1, :, lanes] = jnp.where(key_at <= row_at, 0.0, HIDDEN)
    acc[...] = jnp.zeros_like(acc)
    for copy in copies:
        copy.wait()

    lane_rows = rows // width

    def document_row(block):
        tail = segs[block].astype(F32)
        return jnp.concatenate([tail[r : r + 1, :] for r in range(lane_rows)], axis=1)

    names = lax.broadcasted_iota(jnp.int32, (width, rows), 0).astype(F32)
    for block in range(2 * plane):
        docs = document_row(block)
        hot = jnp.where(names == docs, 1.0, 0.0)
        ka[block, :, width:] = hot.T.astype(BF16)
        last = jnp.max(docs)
        lims[0, block] = jnp.min(docs)
        lims[1, block] = jnp.where(device >= plane, last, -1.0) if block < plane else last

    def folded(values):
        return values.reshape(rows // 8, 8, span)

    def one_block(a, carry):
        first = lims[0, plane + a]
        skip = sum((lims[1, a + b] < first).astype(jnp.int32) for b in range(plane))
        both = qq[a].astype(F32).T.astype(BF16)
        qt[...] = both
        qa[:width, :] = both[:width, :]
        docs = document_row(plane + a)
        cover = jnp.where(names == docs, 0.0, HIDDEN).astype(BF16)
        for g in range(group):
            qa[width:, g * rows : (g + 1) * rows] = cover
        dt[...] = do[a].astype(F32).T.astype(BF16)

        def score(b, bias, top):
            value = jnp.dot(ka[a + b], qa[...], preferred_element_type=F32)
            if bias is not None:
                value = value + tri[bias]
            s[b] = value
            return jnp.maximum(top, jnp.max(folded(value), axis=0))

        top = jnp.full((8, span), HIDDEN, F32)
        top = score(plane, 1, top)
        top = lax.fori_loop(jnp.maximum(skip, 1), plane, lambda b, t: score(b, None, t), top)
        top = lax.cond(skip == 0, lambda t: score(0, 0, t), lambda t: t, top)
        peak = slope * jnp.max(top, axis=0, keepdims=True)

        def sums(b, carry):
            total, dots, ups, both = carry
            weight = jnp.exp2(slope * s[b] - peak)
            s[b] = weight
            dot = factor * jnp.dot(kd[a + b], qt[...], preferred_element_type=F32)
            sd[b] = dot
            up = jnp.dot(vv[a + b, 0], dt[...], preferred_element_type=F32)
            u[b] = up
            updot = jnp.dot(vv[a + b, 1], dt[...], preferred_element_type=F32)
            ud[b] = updot
            total = total + jnp.sum(folded(weight), axis=0)
            dots = dots + jnp.sum(folded(weight * dot), axis=0)
            ups = ups + jnp.sum(folded(weight * up), axis=0)
            both = both + jnp.sum(folded(weight * (dot * up + updot)), axis=0)
            return total, dots, ups, both

        zero = jnp.zeros((8, span), F32)
        carried = lax.fori_loop(skip, plane + 1, sums, (zero, zero, zero, zero))
        total, dots, ups, both = (jnp.sum(x, axis=0, keepdims=True) for x in carried)
        share = 1.0 / total
        mean_dot = dots * share
        center = ups * share
        center_dot = both * share - mean_dot * center

        def adjoints(b, carry):
            mix = s[b] * share
            dot = sd[b] - mean_dot
            up = u[b] - center
            mix_dot = mix * dot
            grad = mix * up
            grad_dot = mix * (dot * up + (ud[b] - center_dot))
            mix_b, mix_dot_b = mix.astype(BF16), mix_dot.astype(BF16)
            grad_b, grad_dot_b = grad.astype(BF16), grad_dot.astype(BF16)
            cot = do[a]
            pair = jnp.dot(grad_b, qq[a], preferred_element_type=F32)
            acc[a + b, 0] += pair[:, :width]
            acc[a + b, 1] += jnp.dot(mix_b, cot, preferred_element_type=F32)
            acc[a + b, 2] += pair[:, width:] + jnp.dot(
                grad_dot_b, qq[a, :, :width], preferred_element_type=F32
            )
            acc[a + b, 3] += jnp.dot(mix_dot_b, cot, preferred_element_type=F32)
            return carry

        lax.fori_loop(skip, plane + 1, adjoints, 0)
        return carry

    lax.fori_loop(0, plane, one_block, 0)
    for k in range(plane):
        for t in range(4):
            scale = factor if t % 2 == 0 else 1.0
            at = slice(t * rows, (t + 1) * rows)
            there = slice((k % half * 4 + t) * rows, (k % half * 4 + t + 1) * rows)
            out_prev[k // half][there, :] = (scale * acc[me ^ k, t]).astype(BF16)
            out_own[k][at, :] = scale * acc[plane + (me ^ k), t]


def attend(own, pairs, queries, plane, group, head):
    length, width = own[1].shape
    rows = (length - TAIL) // 4
    span = group * rows
    vmem = pl.BlockSpec(memory_space=pltpu.VMEM)
    blocks = 2 * plane
    results = pl.pallas_call(
        functools.partial(attend_kernel, plane, group, rows, width, head),
        out_shape=[jax.ShapeDtypeStruct((2 * plane * rows, width), BF16)] * 2
        + [jax.ShapeDtypeStruct((4 * rows, width), F32)] * plane,
        in_specs=[pl.BlockSpec(memory_space=pl.ANY)] * (2 * plane + 2),
        out_specs=[vmem] * (plane + 2),
        scratch_shapes=[
            pltpu.VMEM((blocks, rows, 2 * width), BF16),
            pltpu.VMEM((blocks, rows, 2 * width), BF16),
            pltpu.VMEM((blocks, 2, rows, width), BF16),
            pltpu.VMEM((blocks, TAIL, width), BF16),
            pltpu.VMEM((plane, span, 2 * width), BF16),
            pltpu.VMEM((plane, span, width), BF16),
            pltpu.VMEM((2 * width, span), BF16),
            pltpu.VMEM((2 * width, span), BF16),
            pltpu.VMEM((width, span), BF16),
        ]
        + [pltpu.VMEM((plane + 1, rows, span), F32)] * 4
        + [
            pltpu.VMEM((blocks, 4, rows, width), F32),
            pltpu.VMEM((2, rows, span), F32),
            pltpu.SMEM((2, blocks), F32),
            pltpu.SemaphoreType.DMA((15 * plane,)),
        ],
        name="attend",
    )(*own, *pairs, *queries)
    return results[:2], results[2:]


def finish_kernel(plane, heads, *refs):
    pieces, returned = refs[: plane * heads], refs[plane * heads : plane * heads + heads]
    outs = refs[-4:]
    me = lax.rem(lax.axis_index("ctx"), plane)
    rows = pieces[0].shape[1]
    for h in range(heads):
        for k in range(plane):
            piece = pieces[h * plane + k]
            head = (me ^ k) * heads + h
            for t in range(4):
                value = piece[t].astype(F32)
                if k == 0:
                    value = value + returned[h][t].astype(F32)
                outs[t][pl.ds(head, rows, stride=plane * heads), :] = value


def finish(pieces, returned, plane, heads):
    width = pieces[0].shape[1]
    rows = pieces[0].shape[0] // 4
    steps = 4
    tile = rows // steps
    stacked = [x.reshape(-1, rows, width) for x in list(pieces) + list(returned)]
    return pl.pallas_call(
        functools.partial(finish_kernel, plane, heads),
        grid=(steps,),
        out_shape=[jax.ShapeDtypeStruct((rows * plane * heads, width), F32)] * 4,
        in_specs=[pl.BlockSpec((4, tile, width), lambda i: (0, i, 0))] * len(stacked),
        out_specs=[pl.BlockSpec((tile * plane * heads, width), lambda i: (i, 0))] * 4,
        name="finish",
    )(*stacked)


def local(
    query, query_tangent, keys, values, key_direction, value_direction, out_cotangent, segment_ids
):
    rows, kv_heads, width = keys.shape
    group = query.shape[1] // kv_heads
    plane = WINDOW_LENGTH // rows
    half = plane // 2
    heads = kv_heads // plane
    far_first = list(range(half, plane)) + list(range(1, half))

    def spread(blocks, h):
        results = [blocks[0]] + [None] * (plane - 1)
        for k in far_first:
            results[k] = swapped(blocks[h * (plane - 1) + k], k)
        return results

    seg = segment_ids.reshape(rows // width, width)
    kv = pack((keys, values, key_direction, value_direction), plane, heads, 1, seg)
    qs = pack((query, query_tangent, out_cotangent), plane, heads, group)
    first = shifted(kv[0], plane)
    pieces, returned = [], []
    for h in range(heads):
        own = spread(kv, h)
        pairs = [first, shifted(jnp.concatenate(own[1:], axis=0), plane)]
        queries = spread(qs, h)
        sums_prev, sums_own = attend(own, pairs, queries, plane, group, h)
        back = [None, None]
        for i in (1, 0):
            back[i] = shifted(sums_prev[i], -plane)
        returned.append(back[0])
        totals = [sums_own[0]]
        for k in range(1, plane):
            at = slice(k % half * 4 * rows, (k % half + 1) * 4 * rows)
            totals.append((sums_own[k] + back[k // half][at].astype(F32)).astype(BF16))
        results = [totals[0]] + [None] * (plane - 1)
        for k in far_first:
            results[k] = swapped(totals[k], k)
        pieces.extend(results)
    outs = finish(pieces, returned, plane, heads)
    return tuple(out.reshape(rows, kv_heads, width) for out in outs)


def solution(mesh):
    whole = P(("groups", "ctx"), None, None)
    return jax.shard_map(
        local,
        mesh=mesh,
        in_specs=(whole,) * 7 + (P(("groups", "ctx")),),
        out_specs=(whole,) * 4,
        check_vma=False,
    )
```

```python
import functools

import jax
import jax.numpy as jnp
from jax import lax
from jax.experimental import pallas as pl
from jax.experimental.pallas import tpu as pltpu
from jax.sharding import PartitionSpec as P


WINDOW_LENGTH = 1024
HIDDEN = -1e30
TAIL = 16
F32 = jnp.float32
BF16 = jnp.bfloat16


def shifted(block, distance):
    devices = range(lax.axis_size("ctx"))
    route = [(i, i + distance) for i in devices if i + distance in devices]
    return lax.ppermute(block, "ctx", route)


def swapped(block, partner):
    devices = range(lax.axis_size("ctx"))
    return lax.ppermute(block, "ctx", [(i, i ^ partner) for i in devices])


def pack_kernel(plane, heads, group, arrays, *refs):
    seg = refs[arrays] if group == 1 else None
    outs, wide = refs[-2 - (plane - 1) * heads : -1], refs[-1]
    length = outs[1].shape[0]
    me = lax.rem(lax.axis_index("ctx"), plane)
    for t, array in enumerate(refs[:arrays]):
        rows, count, _ = array.shape
        pitch = count + 1
        values = array[...].astype(F32)
        for r in range(rows):
            wide[r * pitch : r * pitch + count, :] = values[r]
        for h in range(heads):
            for k in range(plane):
                first = ((me ^ k) * heads + h) * group
                out = outs[0] if k == 0 else outs[h * (plane - 1) + k]
                for g in range(group):
                    at = (t * group + g) * rows + (h * length if k == 0 else 0)
                    out[at : at + rows, :] = wide[
                        pl.ds(first + g, rows, stride=pitch), :
                    ].astype(BF16)
    if group == 1:
        docs = seg[...].astype(F32)
        filler = jnp.zeros((TAIL - docs.shape[0], docs.shape[1]), F32)
        tail = jnp.concatenate([docs, filler], axis=0).astype(BF16)
        for h in range(heads):
            outs[0][(h + 1) * length - TAIL : (h + 1) * length, :] = tail
        for out in outs[1:]:
            out[length - TAIL :, :] = tail


def pack(arrays, plane, heads, group, seg=None):
    rows, count, width = arrays[0].shape
    length = len(arrays) * group * rows + (0 if seg is None else TAIL)
    vmem = pl.BlockSpec(memory_space=pltpu.VMEM)
    inputs = list(arrays) + ([] if seg is None else [seg])
    pieces = (plane - 1) * heads
    return pl.pallas_call(
        functools.partial(pack_kernel, plane, heads, group, len(arrays)),
        out_shape=[jax.ShapeDtypeStruct((heads * length, width), BF16)]
        + [jax.ShapeDtypeStruct((length, width), BF16)] * pieces,
        in_specs=[vmem] * len(inputs),
        out_specs=[vmem] * (1 + pieces),
        scratch_shapes=[pltpu.VMEM((rows * (count + 1), width), F32)],
        name="pack",
    )(*inputs)


def attend_kernel(plane, group, rows, width, head, *refs):
    half = plane // 2
    length = 4 * rows + TAIL
    own, pairs, queries = refs[:plane], refs[plane : plane + 2], refs[plane + 2 : 2 * plane + 2]
    out_prev, out_own = refs[2 * plane + 2 : 2 * plane + 4], refs[2 * plane + 4 : 3 * plane + 4]
    ka, kd, vv, segs, qq, do, qt, qa, dt, s, sd, u, ud, acc, tri, lims, sem = refs[3 * plane + 4 :]
    device = lax.axis_index("ctx")
    me = lax.rem(device, plane)
    span = group * rows
    factor = width ** (-0.5)
    slope = factor * 1.4426950408889634

    copies = []

    def fetch(source, target):
        copy = pltpu.make_async_copy(source, target, sem.at[len(copies)])
        copy.start()
        copies.append(copy)

    low, high = pl.ds(0, width), pl.ds(width, width)
    for k in range(plane):
        mine = (own[k], head * length if k == 0 else 0, plane)
        past = (pairs[min(k, 1)], (head if k == 0 else k - 1) * length, 0)
        for piece, start, base in (mine, past):
            block = base + (me ^ k)
            part = [piece.at[pl.ds(start + t * rows, rows), :] for t in range(4)]
            fetch(part[0], ka.at[block, :, low])
            fetch(part[0], kd.at[block, :, high])
            fetch(part[1], vv.at[block, 0])
            fetch(part[2], kd.at[block, :, low])
            fetch(part[3], vv.at[block, 1])
            fetch(piece.at[pl.ds(start + 4 * rows, TAIL), :], segs.at[block])
        block = me ^ k
        start = head * 3 * span if k == 0 else 0
        part = [queries[k].at[pl.ds(start + t * span, span), :] for t in range(3)]
        fetch(part[0], qq.at[block, :, low])
        fetch(part[1], qq.at[block, :, high])
        fetch(part[2], do.at[block])
    key_at = lax.broadcasted_iota(jnp.int32, (rows, rows), 0)
    row_at = lax.broadcasted_iota(jnp.int32, (rows, rows), 1)
    for g in range(group):
        lanes = slice(g * rows, (g + 1) * rows)
        tri[0, :, lanes] = jnp.where(key_at > row_at, 0.0, HIDDEN)
        tri[1, :, lanes] = jnp.where(key_at <= row_at, 0.0, HIDDEN)
    acc[...] = jnp.zeros_like(acc)
    for copy in copies:
        copy.wait()

    lane_rows = rows // width

    def document_row(block):
        tail = segs[block].astype(F32)
        return jnp.concatenate([tail[r : r + 1, :] for r in range(lane_rows)], axis=1)

    names = lax.broadcasted_iota(jnp.int32, (width, rows), 0).astype(F32)
    for block in range(2 * plane):
        docs = document_row(block)
        hot = jnp.where(names == docs, 1.0, 0.0)
        ka[block, :, width:] = hot.T.astype(BF16)
        last = jnp.max(docs)
        lims[0, block] = jnp.min(docs)
        lims[1, block] = jnp.where(device >= plane, last, -1.0) if block < plane else last

    def folded(values):
        return values.reshape(rows // 8, 8, span)

    def one_block(a, carry):
        first = lims[0, plane + a]
        skip = sum((lims[1, a + b] < first).astype(jnp.int32) for b in range(plane))
        both = qq[a].astype(F32).T.astype(BF16)
        qt[...] = both
        qa[:width, :] = both[:width, :]
        docs = document_row(plane + a)
        cover = jnp.where(names == docs, 0.0, HIDDEN).astype(BF16)
        for g in range(group):
            qa[width:, g * rows : (g + 1) * rows] = cover
        dt[...] = do[a].astype(F32).T.astype(BF16)

        def score(b, bias, top):
            value = jnp.dot(ka[a + b], qa[...], preferred_element_type=F32)
            if bias is not None:
                value = value + tri[bias]
            s[b] = value
            return jnp.maximum(top, jnp.max(folded(value), axis=0))

        top = jnp.full((8, span), HIDDEN, F32)
        top = score(plane, 1, top)
        top = lax.fori_loop(jnp.maximum(skip, 1), plane, lambda b, t: score(b, None, t), top)
        top = lax.cond(skip == 0, lambda t: score(0, 0, t), lambda t: t, top)
        peak = slope * jnp.max(top, axis=0, keepdims=True)

        def sums(b, carry):
            total, dots, ups, both = carry
            weight = jnp.exp2(slope * s[b] - peak)
            s[b] = weight
            dot = factor * jnp.dot(kd[a + b], qt[...], preferred_element_type=F32)
            sd[b] = dot
            up = jnp.dot(vv[a + b, 0], dt[...], preferred_element_type=F32)
            u[b] = up
            updot = jnp.dot(vv[a + b, 1], dt[...], preferred_element_type=F32)
            ud[b] = updot
            total = total + jnp.sum(folded(weight), axis=0)
            dots = dots + jnp.sum(folded(weight * dot), axis=0)
            ups = ups + jnp.sum(folded(weight * up), axis=0)
            both = both + jnp.sum(folded(weight * (dot * up + updot)), axis=0)
            return total, dots, ups, both

        zero = jnp.zeros((8, span), F32)
        carried = lax.fori_loop(skip, plane + 1, sums, (zero, zero, zero, zero))
        total, dots, ups, both = (jnp.sum(x, axis=0, keepdims=True) for x in carried)
        share = 1.0 / total
        mean_dot = dots * share
        center = ups * share
        center_dot = both * share - mean_dot * center

        def adjoints(b, carry):
            mix = s[b] * share
            dot = sd[b] - mean_dot
            up = u[b] - center
            mix_dot = mix * dot
            grad = mix * up
            grad_dot = mix * (dot * up + (ud[b] - center_dot))
            mix_b, mix_dot_b = mix.astype(BF16), mix_dot.astype(BF16)
            grad_b, grad_dot_b = grad.astype(BF16), grad_dot.astype(BF16)
            cot = do[a]
            pair = jnp.dot(grad_b, qq[a], preferred_element_type=F32)
            acc[a + b, 0] += pair[:, :width]
            acc[a + b, 1] += jnp.dot(mix_b, cot, preferred_element_type=F32)
            acc[a + b, 2] += pair[:, width:] + jnp.dot(
                grad_dot_b, qq[a, :, :width], preferred_element_type=F32
            )
            acc[a + b, 3] += jnp.dot(mix_dot_b, cot, preferred_element_type=F32)
            return carry

        lax.fori_loop(skip, plane + 1, adjoints, 0)
        return carry

    lax.fori_loop(0, plane, one_block, 0)
    for k in range(plane):
        for t in range(4):
            scale = factor if t % 2 == 0 else 1.0
            at = slice(t * rows, (t + 1) * rows)
            there = slice((k % half * 4 + t) * rows, (k % half * 4 + t + 1) * rows)
            out_prev[k // half][there, :] = (scale * acc[me ^ k, t]).astype(BF16)
            out_own[k][at, :] = scale * acc[plane + (me ^ k), t]


def attend(own, pairs, queries, plane, group, head):
    length, width = own[1].shape
    rows = (length - TAIL) // 4
    span = group * rows
    vmem = pl.BlockSpec(memory_space=pltpu.VMEM)
    blocks = 2 * plane
    results = pl.pallas_call(
        functools.partial(attend_kernel, plane, group, rows, width, head),
        out_shape=[jax.ShapeDtypeStruct((2 * plane * rows, width), BF16)] * 2
        + [jax.ShapeDtypeStruct((4 * rows, width), F32)] * plane,
        in_specs=[pl.BlockSpec(memory_space=pl.ANY)] * (2 * plane + 2),
        out_specs=[vmem] * (plane + 2),
        scratch_shapes=[
            pltpu.VMEM((blocks, rows, 2 * width), BF16),
            pltpu.VMEM((blocks, rows, 2 * width), BF16),
            pltpu.VMEM((blocks, 2, rows, width), BF16),
            pltpu.VMEM((blocks, TAIL, width), BF16),
            pltpu.VMEM((plane, span, 2 * width), BF16),
            pltpu.VMEM((plane, span, width), BF16),
            pltpu.VMEM((2 * width, span), BF16),
            pltpu.VMEM((2 * width, span), BF16),
            pltpu.VMEM((width, span), BF16),
        ]
        + [pltpu.VMEM((plane + 1, rows, span), F32)] * 4
        + [
            pltpu.VMEM((blocks, 4, rows, width), F32),
            pltpu.VMEM((2, rows, span), F32),
            pltpu.SMEM((2, blocks), F32),
            pltpu.SemaphoreType.DMA((15 * plane,)),
        ],
        compiler_params=pltpu.CompilerParams(vmem_limit_bytes=32 << 20),
        name="attend",
    )(*own, *pairs, *queries)
    return results[:2], results[2:]


def finish_kernel(plane, heads, *refs):
    pieces, returned = refs[: plane * heads], refs[plane * heads : plane * heads + heads]
    outs, wide = refs[-5:-1], refs[-1]
    me = lax.rem(lax.axis_index("ctx"), plane)
    rows = pieces[0].shape[1]
    count = plane * heads
    pitch = count + 1
    for h in range(heads):
        for k in range(plane):
            piece = pieces[h * plane + k]
            head = (me ^ k) * heads + h
            for t in range(4):
                value = piece[t].astype(F32)
                if k == 0:
                    value = value + returned[h][t].astype(F32)
                wide[t, pl.ds(head, rows, stride=pitch), :] = value
    for t in range(4):
        for r in range(rows):
            at = slice(r * count, (r + 1) * count)
            outs[t][at, :] = wide[t, r * pitch : r * pitch + count, :]


def finish(pieces, returned, plane, heads):
    width = pieces[0].shape[1]
    rows = pieces[0].shape[0] // 4
    steps = 4
    tile = rows // steps
    stacked = [x.reshape(-1, rows, width) for x in list(pieces) + list(returned)]
    return pl.pallas_call(
        functools.partial(finish_kernel, plane, heads),
        grid=(steps,),
        out_shape=[jax.ShapeDtypeStruct((rows * plane * heads, width), F32)] * 4,
        in_specs=[pl.BlockSpec((4, tile, width), lambda i: (0, i, 0))] * len(stacked),
        out_specs=[pl.BlockSpec((tile * plane * heads, width), lambda i: (i, 0))] * 4,
        scratch_shapes=[pltpu.VMEM((4, tile * (plane * heads + 1), width), F32)],
        name="finish",
    )(*stacked)


def local(
    query, query_tangent, keys, values, key_direction, value_direction, out_cotangent, segment_ids
):
    rows, kv_heads, width = keys.shape
    group = query.shape[1] // kv_heads
    plane = WINDOW_LENGTH // rows
    half = plane // 2
    heads = kv_heads // plane
    far_first = list(range(half, plane)) + list(range(1, half))

    def spread(blocks, h):
        results = [blocks[0]] + [None] * (plane - 1)
        for k in far_first:
            results[k] = swapped(blocks[h * (plane - 1) + k], k)
        return results

    seg = segment_ids.reshape(rows // width, width)
    kv = pack((keys, values, key_direction, value_direction), plane, heads, 1, seg)
    qs = pack((query, query_tangent, out_cotangent), plane, heads, group)
    first = shifted(kv[0], plane)
    pieces, returned = [], []
    for h in range(heads):
        own = spread(kv, h)
        pairs = [first, shifted(jnp.concatenate(own[1:], axis=0), plane)]
        queries = spread(qs, h)
        sums_prev, sums_own = attend(own, pairs, queries, plane, group, h)
        back = [None, None]
        for i in (1, 0):
            back[i] = shifted(sums_prev[i], -plane)
        returned.append(back[0])
        totals = [sums_own[0]]
        for k in range(1, plane):
            at = slice(k % half * 4 * rows, (k % half + 1) * 4 * rows)
            totals.append((sums_own[k] + back[k // half][at].astype(F32)).astype(BF16))
        results = [totals[0]] + [None] * (plane - 1)
        for k in far_first:
            results[k] = swapped(totals[k], k)
        pieces.extend(results)
    outs = finish(pieces, returned, plane, heads)
    return tuple(out.reshape(rows, kv_heads, width) for out in outs)


def solution(mesh):
    whole = P(("groups", "ctx"), None, None)
    return jax.shard_map(
        local,
        mesh=mesh,
        in_specs=(whole,) * 7 + (P(("groups", "ctx")),),
        out_specs=(whole,) * 4,
        check_vma=False,
    )
```

```python
import functools

import jax
import jax.numpy as jnp
from jax import lax
from jax.experimental import pallas as pl
from jax.experimental.pallas import tpu as pltpu
from jax.sharding import PartitionSpec as P


WINDOW_LENGTH = 1024
HIDDEN = -1e30
TAIL = 16
F32 = jnp.float32
BF16 = jnp.bfloat16


def shifted(block, distance):
    devices = range(lax.axis_size("ctx"))
    route = [(i, i + distance) for i in devices if i + distance in devices]
    return lax.ppermute(block, "ctx", route)


def swapped(block, partner):
    devices = range(lax.axis_size("ctx"))
    return lax.ppermute(block, "ctx", [(i, i ^ partner) for i in devices])


def pack_kernel(plane, heads, group, arrays, *refs):
    seg = refs[arrays] if group == 1 else None
    outs, wide = refs[-2 - (plane - 1) * heads : -1], refs[-1]
    length = outs[1].shape[0]
    me = lax.rem(lax.axis_index("ctx"), plane)
    for t, array in enumerate(refs[:arrays]):
        rows, count, _ = array.shape
        pitch = count + 1
        values = array[...].astype(F32)
        for r in range(rows):
            wide[r * pitch : r * pitch + count, :] = values[r]
        for h in range(heads):
            for k in range(plane):
                first = ((me ^ k) * heads + h) * group
                out = outs[0] if k == 0 else outs[h * (plane - 1) + k]
                for g in range(group):
                    at = (t * group + g) * rows + (h * length if k == 0 else 0)
                    out[at : at + rows, :] = wide[
                        pl.ds(first + g, rows, stride=pitch), :
                    ].astype(BF16)
    if group == 1:
        docs = seg[...].astype(F32)
        filler = jnp.zeros((TAIL - docs.shape[0], docs.shape[1]), F32)
        tail = jnp.concatenate([docs, filler], axis=0).astype(BF16)
        for h in range(heads):
            outs[0][(h + 1) * length - TAIL : (h + 1) * length, :] = tail
        for out in outs[1:]:
            out[length - TAIL :, :] = tail


def pack(arrays, plane, heads, group, seg=None):
    rows, count, width = arrays[0].shape
    length = len(arrays) * group * rows + (0 if seg is None else TAIL)
    vmem = pl.BlockSpec(memory_space=pltpu.VMEM)
    inputs = list(arrays) + ([] if seg is None else [seg])
    pieces = (plane - 1) * heads
    return pl.pallas_call(
        functools.partial(pack_kernel, plane, heads, group, len(arrays)),
        out_shape=[jax.ShapeDtypeStruct((heads * length, width), BF16)]
        + [jax.ShapeDtypeStruct((length, width), BF16)] * pieces,
        in_specs=[vmem] * len(inputs),
        out_specs=[vmem] * (1 + pieces),
        scratch_shapes=[pltpu.VMEM((rows * (count + 1), width), F32)],
        name="pack",
    )(*inputs)


def attend_kernel(plane, group, rows, width, head, picks, begin, end, *refs):
    half = plane // 2
    length = 4 * rows + TAIL
    own, pairs, refs = refs[:plane], refs[plane : plane + 2], refs[plane + 2 :]
    queries, refs = refs[: len(picks)], refs[len(picks) :]
    if not begin:
        start_sums, refs = refs[0], refs[1:]
    if end:
        out_prev, out_own, refs = refs[:2], refs[2 : plane + 2], refs[plane + 2 :]
    else:
        end_sums, refs = refs[0], refs[1:]
    ka, kd, vv, segs, qq, do, qt, qa, dt, s, sd, u, ud, acc, tri, lims, sem = refs
    device = lax.axis_index("ctx")
    me = lax.rem(device, plane)
    span = group * rows
    factor = width ** (-0.5)
    slope = factor * 1.4426950408889634

    copies = []

    def fetch(source, target):
        copy = pltpu.make_async_copy(source, target, sem.at[len(copies)])
        copy.start()
        copies.append(copy)

    low, high = pl.ds(0, width), pl.ds(width, width)
    for k in range(plane):
        mine = (own[k], head * length if k == 0 else 0, plane)
        past = (pairs[min(k, 1)], (head if k == 0 else k - 1) * length, 0)
        for piece, start, base in (mine, past):
            block = base + (me ^ k)
            part = [piece.at[pl.ds(start + t * rows, rows), :] for t in range(4)]
            fetch(part[0], ka.at[block, :, low])
            fetch(part[0], kd.at[block, :, high])
            fetch(part[1], vv.at[block, 0])
            fetch(part[2], kd.at[block, :, low])
            fetch(part[3], vv.at[block, 1])
            fetch(piece.at[pl.ds(start + 4 * rows, TAIL), :], segs.at[block])
    for i, k in enumerate(picks):
        start = head * 3 * span if k == 0 else 0
        part = [queries[i].at[pl.ds(start + t * span, span), :] for t in range(3)]
        fetch(part[0], qq.at[i, :, low])
        fetch(part[1], qq.at[i, :, high])
        fetch(part[2], do.at[i])
    key_at = lax.broadcasted_iota(jnp.int32, (rows, rows), 0)
    row_at = lax.broadcasted_iota(jnp.int32, (rows, rows), 1)
    for g in range(group):
        lanes = slice(g * rows, (g + 1) * rows)
        tri[0, :, lanes] = jnp.where(key_at > row_at, 0.0, HIDDEN)
        tri[1, :, lanes] = jnp.where(key_at <= row_at, 0.0, HIDDEN)
    acc[...] = jnp.zeros_like(acc) if begin else start_sums[...]
    for copy in copies:
        copy.wait()

    lane_rows = rows // width

    def document_row(block):
        tail = segs[block].astype(F32)
        return jnp.concatenate([tail[r : r + 1, :] for r in range(lane_rows)], axis=1)

    names = lax.broadcasted_iota(jnp.int32, (width, rows), 0).astype(F32)
    for block in range(2 * plane):
        docs = document_row(block)
        hot = jnp.where(names == docs, 1.0, 0.0)
        ka[block, :, width:] = hot.T.astype(BF16)
        last = jnp.max(docs)
        lims[0, block] = jnp.min(docs)
        lims[1, block] = jnp.where(device >= plane, last, -1.0) if block < plane else last

    def folded(values):
        return values.reshape(rows // 8, 8, span)

    def one_block(i, carry):
        a = me ^ (picks[0] + i)
        first = lims[0, plane + a]
        skip = sum((lims[1, a + b] < first).astype(jnp.int32) for b in range(plane))
        both = qq[i].astype(F32).T.astype(BF16)
        qt[...] = both
        qa[:width, :] = both[:width, :]
        docs = document_row(plane + a)
        cover = jnp.where(names == docs, 0.0, HIDDEN).astype(BF16)
        for g in range(group):
            qa[width:, g * rows : (g + 1) * rows] = cover
        dt[...] = do[i].astype(F32).T.astype(BF16)

        def score(b, bias, top):
            value = jnp.dot(ka[a + b], qa[...], preferred_element_type=F32)
            if bias is not None:
                value = value + tri[bias]
            s[b] = value
            return jnp.maximum(top, jnp.max(folded(value), axis=0))

        top = jnp.full((8, span), HIDDEN, F32)
        top = score(plane, 1, top)
        top = lax.fori_loop(jnp.maximum(skip, 1), plane, lambda b, t: score(b, None, t), top)
        top = lax.cond(skip == 0, lambda t: score(0, 0, t), lambda t: t, top)
        peak = slope * jnp.max(top, axis=0, keepdims=True)

        def sums(b, carry):
            total, dots, ups, both = carry
            weight = jnp.exp2(slope * s[b] - peak)
            s[b] = weight
            dot = factor * jnp.dot(kd[a + b], qt[...], preferred_element_type=F32)
            sd[b] = dot
            up = jnp.dot(vv[a + b, 0], dt[...], preferred_element_type=F32)
            u[b] = up
            updot = jnp.dot(vv[a + b, 1], dt[...], preferred_element_type=F32)
            ud[b] = updot
            total = total + jnp.sum(folded(weight), axis=0)
            dots = dots + jnp.sum(folded(weight * dot), axis=0)
            ups = ups + jnp.sum(folded(weight * up), axis=0)
            both = both + jnp.sum(folded(weight * (dot * up + updot)), axis=0)
            return total, dots, ups, both

        zero = jnp.zeros((8, span), F32)
        carried = lax.fori_loop(skip, plane + 1, sums, (zero, zero, zero, zero))
        total, dots, ups, both = (jnp.sum(x, axis=0, keepdims=True) for x in carried)
        share = 1.0 / total
        mean_dot = dots * share
        center = ups * share
        center_dot = both * share - mean_dot * center

        def adjoints(b, carry):
            mix = s[b] * share
            dot = sd[b] - mean_dot
            up = u[b] - center
            mix_dot = mix * dot
            grad = mix * up
            grad_dot = mix * (dot * up + (ud[b] - center_dot))
            mix_b, mix_dot_b = mix.astype(BF16), mix_dot.astype(BF16)
            grad_b, grad_dot_b = grad.astype(BF16), grad_dot.astype(BF16)
            cot = do[i]
            pair = jnp.dot(grad_b, qq[i], preferred_element_type=F32)
            acc[a + b, 0] += pair[:, :width]
            acc[a + b, 1] += jnp.dot(mix_b, cot, preferred_element_type=F32)
            acc[a + b, 2] += pair[:, width:] + jnp.dot(
                grad_dot_b, qq[i, :, :width], preferred_element_type=F32
            )
            acc[a + b, 3] += jnp.dot(mix_dot_b, cot, preferred_element_type=F32)
            return carry

        lax.fori_loop(skip, plane + 1, adjoints, 0)
        return carry

    lax.fori_loop(0, len(picks), one_block, 0)
    if not end:
        end_sums[...] = acc[...]
        return
    for k in range(plane):
        for t in range(4):
            scale = factor if t % 2 == 0 else 1.0
            at = slice(t * rows, (t + 1) * rows)
            there = slice((k % half * 4 + t) * rows, (k % half * 4 + t + 1) * rows)
            out_prev[k // half][there, :] = (scale * acc[me ^ k, t]).astype(BF16)
            out_own[k][at, :] = scale * acc[plane + (me ^ k), t]


def attend(own, pairs, queries, plane, group, head, picks, sums=None, end=True):
    length, width = own[1].shape
    rows = (length - TAIL) // 4
    span = group * rows
    vmem = pl.BlockSpec(memory_space=pltpu.VMEM)
    blocks = 2 * plane
    begin = sums is None
    if end:
        out_shape = [jax.ShapeDtypeStruct((2 * plane * rows, width), BF16)] * 2
        out_shape += [jax.ShapeDtypeStruct((4 * rows, width), F32)] * plane
    else:
        out_shape = [pltpu.VMEM((blocks, 4, rows, width), F32)]
    inputs = [*own, *pairs, *queries]
    in_specs = [pl.BlockSpec(memory_space=pl.ANY)] * len(inputs)
    if not begin:
        inputs.append(pltpu.with_memory_space_constraint(sums, pltpu.VMEM))
        in_specs.append(vmem)
    results = pl.pallas_call(
        functools.partial(
            attend_kernel, plane, group, rows, width, head, tuple(picks), begin, end
        ),
        out_shape=out_shape,
        in_specs=in_specs,
        out_specs=[vmem] * len(out_shape),
        scratch_shapes=[
            pltpu.VMEM((blocks, rows, 2 * width), BF16),
            pltpu.VMEM((blocks, rows, 2 * width), BF16),
            pltpu.VMEM((blocks, 2, rows, width), BF16),
            pltpu.VMEM((blocks, TAIL, width), BF16),
            pltpu.VMEM((len(picks), span, 2 * width), BF16),
            pltpu.VMEM((len(picks), span, width), BF16),
            pltpu.VMEM((2 * width, span), BF16),
            pltpu.VMEM((2 * width, span), BF16),
            pltpu.VMEM((width, span), BF16),
        ]
        + [pltpu.VMEM((plane + 1, rows, span), F32)] * 4
        + [
            pltpu.VMEM((blocks, 4, rows, width), F32),
            pltpu.VMEM((2, rows, span), F32),
            pltpu.SMEM((2, blocks), F32),
            pltpu.SemaphoreType.DMA((12 * plane + 3 * len(picks),)),
        ],
        compiler_params=pltpu.CompilerParams(vmem_limit_bytes=32 << 20),
        name="attend",
    )(*inputs)
    return (results[:2], results[2:]) if end else results[0]


def finish_kernel(plane, heads, tile, *refs):
    pieces, returned = refs[: plane * heads], refs[plane * heads : plane * heads + heads]
    outs, wide = refs[-5:-1], refs[-1]
    me = lax.rem(lax.axis_index("ctx"), plane)
    count = plane * heads
    pitch = count + 1
    here = pl.ds(pl.multiple_of(pl.program_id(0) * tile, tile), tile)
    for h in range(heads):
        for k in range(plane):
            head = (me ^ k) * heads + h
            for t in range(4):
                value = pieces[h * plane + k][t, here, :].astype(F32)
                if k == 0:
                    value = value + returned[h][t, here, :].astype(F32)
                wide[t, pl.ds(head, tile, stride=pitch), :] = value
    for t in range(4):
        for r in range(tile):
            at = slice(r * count, (r + 1) * count)
            outs[t][at, :] = wide[t, r * pitch : r * pitch + count, :]


def finish(pieces, returned, plane, heads):
    width = pieces[0].shape[1]
    rows = pieces[0].shape[0] // 4
    steps = 4
    tile = rows // steps
    stacked = [x.reshape(-1, rows, width) for x in list(pieces) + list(returned)]
    stacked = [pltpu.with_memory_space_constraint(x, pltpu.VMEM) for x in stacked]
    return pl.pallas_call(
        functools.partial(finish_kernel, plane, heads, tile),
        grid=(steps,),
        out_shape=[jax.ShapeDtypeStruct((rows * plane * heads, width), F32)] * 4,
        in_specs=[pl.BlockSpec(memory_space=pltpu.VMEM)] * len(stacked),
        out_specs=[pl.BlockSpec((tile * plane * heads, width), lambda i: (i, 0))] * 4,
        scratch_shapes=[pltpu.VMEM((4, tile * (plane * heads + 1), width), F32)],
        compiler_params=pltpu.CompilerParams(vmem_limit_bytes=24 << 20),
        name="finish",
    )(*stacked)


def local(
    query, query_tangent, keys, values, key_direction, value_direction, out_cotangent, segment_ids
):
    rows, kv_heads, width = keys.shape
    group = query.shape[1] // kv_heads
    plane = WINDOW_LENGTH // rows
    half = plane // 2
    heads = kv_heads // plane
    far_first = list(range(half, plane)) + list(range(1, half))

    def spread(blocks, h):
        results = [blocks[0]] + [None] * (plane - 1)
        for k in far_first:
            results[k] = swapped(blocks[h * (plane - 1) + k], k)
        return results

    seg = segment_ids.reshape(rows // width, width)
    kv = pack((keys, values, key_direction, value_direction), plane, heads, 1, seg)
    qs = pack((query, query_tangent, out_cotangent), plane, heads, group)
    first = shifted(kv[0], plane)
    pieces, returned = [], []
    for h in range(heads):
        own = spread(kv, h)
        pairs = [first, shifted(jnp.concatenate(own[1:], axis=0), plane)]
        queries = spread(qs, h)
        near, far, every = range(half), range(half, plane), range(plane)
        if h == 0:
            sums = attend(own, pairs, queries[:half], plane, group, h, near, end=False)
            sums_prev, sums_own = attend(own, pairs, queries[half:], plane, group, h, far, sums)
        else:
            sums_prev, sums_own = attend(own, pairs, queries, plane, group, h, every)
        back = [None, None]
        for i in (1, 0):
            back[i] = shifted(sums_prev[i], -plane)
        returned.append(back[0])
        totals = [sums_own[0]]
        for k in range(1, plane):
            at = slice(k % half * 4 * rows, (k % half + 1) * 4 * rows)
            totals.append((sums_own[k] + back[k // half][at].astype(F32)).astype(BF16))
        results = [totals[0]] + [None] * (plane - 1)
        for k in far_first:
            results[k] = swapped(totals[k], k)
        pieces.extend(results)
    outs = finish(pieces, returned, plane, heads)
    return tuple(out.reshape(rows, kv_heads, width) for out in outs)


def solution(mesh):
    whole = P(("groups", "ctx"), None, None)
    return jax.shard_map(
        local,
        mesh=mesh,
        in_specs=(whole,) * 7 + (P(("groups", "ctx")),),
        out_specs=(whole,) * 4,
        check_vma=False,
    )
```

```python
import functools

import jax
import jax.numpy as jnp
from jax import lax
from jax.experimental import pallas as pl
from jax.experimental.pallas import tpu as pltpu
from jax.sharding import PartitionSpec as P


WINDOW_LENGTH = 1024
HIDDEN = -1e30
TAIL = 16
F32 = jnp.float32
BF16 = jnp.bfloat16


def shifted(block, distance):
    devices = range(lax.axis_size("ctx"))
    route = [(i, i + distance) for i in devices if i + distance in devices]
    return lax.ppermute(block, "ctx", route)


def swapped(block, partner):
    devices = range(lax.axis_size("ctx"))
    return lax.ppermute(block, "ctx", [(i, i ^ partner) for i in devices])


def pack_kernel(plane, heads, group, arrays, *refs):
    seg = refs[arrays] if group == 1 else None
    outs, wide = refs[-1 - plane * heads : -1], refs[-1]
    length = outs[0].shape[0]
    me = lax.rem(lax.axis_index("ctx"), plane)
    for t, array in enumerate(refs[:arrays]):
        rows, count, _ = array.shape
        pitch = count + 1
        values = array[...].astype(F32)
        for r in range(rows):
            wide[r * pitch : r * pitch + count, :] = values[r]
        for h in range(heads):
            for k in range(plane):
                first = ((me ^ k) * heads + h) * group
                for g in range(group):
                    at = (t * group + g) * rows
                    outs[h * plane + k][at : at + rows, :] = wide[
                        pl.ds(first + g, rows, stride=pitch), :
                    ].astype(BF16)
    if group == 1:
        docs = seg[...].astype(F32)
        filler = jnp.zeros((TAIL - docs.shape[0], docs.shape[1]), F32)
        tail = jnp.concatenate([docs, filler], axis=0).astype(BF16)
        for out in outs:
            out[length - TAIL :, :] = tail


def pack(arrays, plane, heads, group, seg=None):
    rows, count, width = arrays[0].shape
    length = len(arrays) * group * rows + (0 if seg is None else TAIL)
    vmem = pl.BlockSpec(memory_space=pltpu.VMEM)
    inputs = list(arrays) + ([] if seg is None else [seg])
    return pl.pallas_call(
        functools.partial(pack_kernel, plane, heads, group, len(arrays)),
        out_shape=[jax.ShapeDtypeStruct((length, width), BF16)] * (plane * heads),
        in_specs=[vmem] * len(inputs),
        out_specs=[vmem] * (plane * heads),
        scratch_shapes=[pltpu.VMEM((rows * (count + 1), width), F32)],
        name="pack",
    )(*inputs)


def attend_kernel(plane, group, rows, width, head, picks, begin, end, *refs):
    half = plane // 2
    length = 4 * rows + TAIL
    own, refs = refs[:plane], refs[plane:]
    came = 2 if head == 0 else 1
    pairs, refs = refs[:came], refs[came:]
    queries, refs = refs[: len(picks)], refs[len(picks) :]
    if not begin:
        start_sums, refs = refs[0], refs[1:]
    if end:
        out_prev, out_own, refs = refs[:2], refs[2 : plane + 2], refs[plane + 2 :]
    else:
        end_sums, refs = refs[0], refs[1:]
    ka, kd, vv, segs, qq, do, qt, qa, dt, s, sd, u, ud, acc, tri, lims, sem = refs
    if not end:
        acc = end_sums
    device = lax.axis_index("ctx")
    me = lax.rem(device, plane)
    span = group * rows
    factor = width ** (-0.5)
    slope = factor * 1.4426950408889634

    copies = []

    def fetch(source, target):
        copy = pltpu.make_async_copy(source, target, sem.at[len(copies)])
        copy.start()
        copies.append(copy)

    low, high = pl.ds(0, width), pl.ds(width, width)
    for k in range(plane):
        mine = (own[k], 0, plane)
        past = (pairs[min(k, came - 1)], max(k - came + 1, 0) * length, 0)
        for piece, start, base in (mine, past):
            block = base + (me ^ k)
            part = [piece.at[pl.ds(start + t * rows, rows), :] for t in range(4)]
            fetch(part[0], ka.at[block, :, low])
            fetch(part[0], kd.at[block, :, high])
            fetch(part[1], vv.at[block, pl.ds(0, rows)])
            fetch(part[2], kd.at[block, :, low])
            fetch(part[3], vv.at[block, pl.ds(rows, rows)])
            fetch(piece.at[pl.ds(start + 4 * rows, TAIL), :], segs.at[block])
    for i, k in enumerate(picks):
        part = [queries[i].at[pl.ds(t * span, span), :] for t in range(3)]
        fetch(part[0], qq.at[i, :, low])
        fetch(part[1], qq.at[i, :, high])
        fetch(part[2], do.at[i])
    key_at = lax.broadcasted_iota(jnp.int32, (rows, rows), 0)
    row_at = lax.broadcasted_iota(jnp.int32, (rows, rows), 1)
    for g in range(group):
        lanes = slice(g * rows, (g + 1) * rows)
        tri[0, :, lanes] = jnp.where(key_at > row_at, 0.0, HIDDEN)
        tri[1, :, lanes] = jnp.where(key_at <= row_at, 0.0, HIDDEN)
    acc[...] = jnp.zeros_like(acc) if begin else start_sums[...]
    for copy in copies:
        copy.wait()

    lane_rows = rows // width

    def document_row(block):
        tail = segs[block].astype(F32)
        return jnp.concatenate([tail[r : r + 1, :] for r in range(lane_rows)], axis=1)

    names = lax.broadcasted_iota(jnp.int32, (width, rows), 0).astype(F32)
    for block in range(2 * plane):
        docs = document_row(block)
        hot = jnp.where(names == docs, 1.0, 0.0)
        ka[block, :, width:] = hot.T.astype(BF16)
        last = jnp.max(docs)
        lims[0, block] = jnp.min(docs)
        lims[1, block] = jnp.where(device >= plane, last, -1.0) if block < plane else last

    def folded(values):
        return values.reshape(rows // 8, 8, span)

    def one_block(i, carry):
        a = me ^ (picks[0] + i)
        first = lims[0, plane + a]
        skip = sum((lims[1, a + b] < first).astype(jnp.int32) for b in range(plane))
        both = qq[i].T
        qt[...] = both
        qa[:width, :] = both[:width, :]
        docs = document_row(plane + a)
        cover = jnp.where(names == docs, 0.0, HIDDEN).astype(BF16)
        for g in range(group):
            qa[width:, g * rows : (g + 1) * rows] = cover
        dt[...] = do[i].T

        def score(b, bias, top):
            value = jnp.dot(ka[a + b], qa[...], preferred_element_type=F32)
            if bias is not None:
                value = value + tri[bias]
            s[b] = value
            return jnp.maximum(top, jnp.max(folded(value), axis=0))

        top = jnp.full((8, span), HIDDEN, F32)
        top = score(plane, 1, top)
        top = lax.fori_loop(jnp.maximum(skip, 1), plane, lambda b, t: score(b, None, t), top)
        top = lax.cond(skip == 0, lambda t: score(0, 0, t), lambda t: t, top)
        peak = slope * jnp.max(top, axis=0, keepdims=True)

        def sums(b, carry):
            total, dots, ups, both = carry
            weight = jnp.exp2(slope * s[b] - peak)
            s[b] = weight
            dot = factor * jnp.dot(kd[a + b], qt[...], preferred_element_type=F32)
            sd[b] = dot
            stacked = jnp.dot(vv[a + b], dt[...], preferred_element_type=F32)
            up, updot = stacked[:rows], stacked[rows:]
            u[b] = up
            ud[b] = updot
            total = total + jnp.sum(folded(weight), axis=0)
            dots = dots + jnp.sum(folded(weight * dot), axis=0)
            ups = ups + jnp.sum(folded(weight * up), axis=0)
            both = both + jnp.sum(folded(weight * (dot * up + updot)), axis=0)
            return total, dots, ups, both

        zero = jnp.zeros((8, span), F32)
        carried = lax.fori_loop(skip, plane + 1, sums, (zero, zero, zero, zero))
        total, dots, ups, both = (jnp.sum(x, axis=0, keepdims=True) for x in carried)
        share = 1.0 / total
        mean_dot = dots * share
        center = ups * share
        center_dot = both * share - mean_dot * center

        def adjoints(b, carry):
            mix = s[b] * share
            dot = sd[b] - mean_dot
            up = u[b] - center
            mix_dot = mix * dot
            grad = mix * up
            grad_dot = mix * (dot * up + (ud[b] - center_dot))
            mix_b, mix_dot_b = mix.astype(BF16), mix_dot.astype(BF16)
            grad_b, grad_dot_b = grad.astype(BF16), grad_dot.astype(BF16)
            cot = do[i]
            pair = jnp.dot(grad_b, qq[i], preferred_element_type=F32)
            acc[a + b, 0] += pair[:, :width]
            acc[a + b, 1] += jnp.dot(mix_b, cot, preferred_element_type=F32)
            acc[a + b, 2] += pair[:, width:] + jnp.dot(
                grad_dot_b, qq[i, :, :width], preferred_element_type=F32
            )
            acc[a + b, 3] += jnp.dot(mix_dot_b, cot, preferred_element_type=F32)
            return carry

        lax.fori_loop(skip, plane + 1, adjoints, 0)
        return carry

    lax.fori_loop(0, len(picks), one_block, 0)
    if not end:
        return
    for k in range(plane):
        for t in range(4):
            scale = factor if t % 2 == 0 else 1.0
            at = slice(t * rows, (t + 1) * rows)
            there = slice((k % half * 4 + t) * rows, (k % half * 4 + t + 1) * rows)
            out_prev[k // half][there, :] = (scale * acc[me ^ k, t]).astype(BF16)
            out_own[k][at, :] = scale * acc[plane + (me ^ k), t]


def attend(own, pairs, queries, plane, group, head, picks, sums=None, end=True):
    length, width = own[1].shape
    rows = (length - TAIL) // 4
    span = group * rows
    vmem = pl.BlockSpec(memory_space=pltpu.VMEM)
    blocks = 2 * plane
    begin = sums is None
    if end:
        out_shape = [jax.ShapeDtypeStruct((2 * plane * rows, width), BF16)] * 2
        out_shape += [jax.ShapeDtypeStruct((4 * rows, width), F32)] * plane
    else:
        out_shape = [pltpu.VMEM((blocks, 4, rows, width), F32)]
    inputs = [*own, *pairs, *queries]
    in_specs = [pl.BlockSpec(memory_space=pl.ANY)] * len(inputs)
    if not begin:
        inputs.append(pltpu.with_memory_space_constraint(sums, pltpu.VMEM))
        in_specs.append(vmem)
    results = pl.pallas_call(
        functools.partial(
            attend_kernel, plane, group, rows, width, head, tuple(picks), begin, end
        ),
        out_shape=out_shape,
        in_specs=in_specs,
        out_specs=[vmem] * len(out_shape),
        scratch_shapes=[
            pltpu.VMEM((blocks, rows, 2 * width), BF16),
            pltpu.VMEM((blocks, rows, 2 * width), BF16),
            pltpu.VMEM((blocks, 2 * rows, width), BF16),
            pltpu.VMEM((blocks, TAIL, width), BF16),
            pltpu.VMEM((len(picks), span, 2 * width), BF16),
            pltpu.VMEM((len(picks), span, width), BF16),
            pltpu.VMEM((2 * width, span), BF16),
            pltpu.VMEM((2 * width, span), BF16),
            pltpu.VMEM((width, span), BF16),
        ]
        + [pltpu.VMEM((plane + 1, rows, span), F32)] * 4
        + [
            pltpu.VMEM((blocks if end else 1, 4, rows, width), F32),
            pltpu.VMEM((2, rows, span), F32),
            pltpu.SMEM((2, blocks), F32),
            pltpu.SemaphoreType.DMA((12 * plane + 3 * len(picks),)),
        ],
        compiler_params=pltpu.CompilerParams(vmem_limit_bytes=32 << 20),
        name="attend",
    )(*inputs)
    return (results[:2], results[2:]) if end else results[0]


def finish_kernel(plane, heads, tile, *refs):
    pieces, returned = refs[: plane * heads], refs[plane * heads : plane * heads + heads]
    outs, wide = refs[-5:-1], refs[-1]
    me = lax.rem(lax.axis_index("ctx"), plane)
    count = plane * heads
    pitch = count + 1
    here = pl.ds(pl.multiple_of(pl.program_id(0) * tile, tile), tile)
    for h in range(heads):
        for k in range(plane):
            head = (me ^ k) * heads + h
            for t in range(4):
                value = pieces[h * plane + k][t, here, :].astype(F32)
                if k == 0:
                    value = value + returned[h][t, here, :].astype(F32)
                wide[t, pl.ds(head, tile, stride=pitch), :] = value
    for t in range(4):
        for r in range(tile):
            at = slice(r * count, (r + 1) * count)
            outs[t][at, :] = wide[t, r * pitch : r * pitch + count, :]


def finish(pieces, returned, plane, heads):
    width = pieces[0].shape[1]
    rows = pieces[0].shape[0] // 4
    steps = 4
    tile = rows // steps
    stacked = [x.reshape(-1, rows, width) for x in list(pieces) + list(returned)]
    stacked = [pltpu.with_memory_space_constraint(x, pltpu.VMEM) for x in stacked]
    return pl.pallas_call(
        functools.partial(finish_kernel, plane, heads, tile),
        grid=(steps,),
        out_shape=[jax.ShapeDtypeStruct((rows * plane * heads, width), F32)] * 4,
        in_specs=[pl.BlockSpec(memory_space=pltpu.VMEM)] * len(stacked),
        out_specs=[pl.BlockSpec((tile * plane * heads, width), lambda i: (i, 0))] * 4,
        scratch_shapes=[pltpu.VMEM((4, tile * (plane * heads + 1), width), F32)],
        compiler_params=pltpu.CompilerParams(vmem_limit_bytes=24 << 20),
        name="finish",
    )(*stacked)


def local(
    query, query_tangent, keys, values, key_direction, value_direction, out_cotangent, segment_ids
):
    rows, kv_heads, width = keys.shape
    group = query.shape[1] // kv_heads
    plane = WINDOW_LENGTH // rows
    half = plane // 2
    heads = kv_heads // plane
    far_first = list(range(half, plane)) + list(range(1, half))

    def spread(blocks, h):
        results = [blocks[h * plane]] + [None] * (plane - 1)
        for k in far_first:
            results[k] = swapped(blocks[h * plane + k], k)
        return results

    seg = segment_ids.reshape(rows // width, width)
    kv = pack((keys, values, key_direction, value_direction), plane, heads, 1, seg)
    qs = pack((query, query_tangent, out_cotangent), plane, heads, group)
    first = [shifted(kv[0], plane)]
    pieces, returned = [], []
    for h in range(heads):
        own = spread(kv, h)
        rest = own[1:] if h == 0 else own
        pairs = (first if h == 0 else []) + [
            shifted(jnp.concatenate(rest, axis=0), plane)
        ]
        queries = spread(qs, h)
        near, far, every = range(half), range(half, plane), range(plane)
        if h == 0:
            sums = attend(own, pairs, queries[:half], plane, group, h, near, end=False)
            sums_prev, sums_own = attend(own, pairs, queries[half:], plane, group, h, far, sums)
        else:
            sums_prev, sums_own = attend(own, pairs, queries, plane, group, h, every)
        back = [None, None]
        for i in (1, 0):
            back[i] = shifted(sums_prev[i], -plane)
        returned.append(back[0])
        totals = [sums_own[0]]
        for k in range(1, plane):
            at = slice(k % half * 4 * rows, (k % half + 1) * 4 * rows)
            totals.append((sums_own[k] + back[k // half][at].astype(F32)).astype(BF16))
        results = [totals[0]] + [None] * (plane - 1)
        for k in far_first:
            results[k] = swapped(totals[k], k)
        pieces.extend(results)
    outs = finish(pieces, returned, plane, heads)
    return tuple(out.reshape(rows, kv_heads, width) for out in outs)


def solution(mesh):
    whole = P(("groups", "ctx"), None, None)
    return jax.shard_map(
        local,
        mesh=mesh,
        in_specs=(whole,) * 7 + (P(("groups", "ctx")),),
        out_specs=(whole,) * 4,
        check_vma=False,
    )
```
